256 devices in a mesh: gx: 16 (over z, core), gy: 4 (over x), af: 4 (over y).
Axes of the slice: x: 4, y: 4, z: 8, core: 2. Of those that a mesh axis runs over, the one named last changes fastest.
Arguments:
- features: bfloat16 [65536, 1024], P(('gx', 'gy'), 'af'), may hold values from -6 to 6
- adj_tiles: bfloat16 [512, 4, 128, 128], P(('gx', 'gy')), may hold values from -0.25 to 0.25
- col_block: int32 [512, 4], P(('gx', 'gy')), may hold values from 0 to 7, as said below
- send_rows: int32 [256, 384], P(('gx', 'gy')), may hold values from 0 to 1023
- send_counts: int32 [256], P(('gx', 'gy')), may hold values from 96 to 384, as said below
- recv_target: int32 [256, 384], P(('gx', 'gy')), may hold values from 0 to 1023
- edge_weight: float32 [256, 384], P(('gx', 'gy')), may hold values from -3 to 3
- labels: int32 [65536], P(('gx', 'gy')), may hold values from 0 to 127
- w_hidden: bfloat16 [1024, 1024], P('af'), may hold values from -0.1875 to 0.1875
- w_classes: bfloat16 [1024, 128], P('af'), may hold values from -0.5 to 0.5
Outputs:
- grad_w_hidden: float32 [1024, 1024], P('af')
- grad_w_classes: float32 [1024, 128], P('af')
The draws below stay inside these ranges and needn't reach their ends.
Inputs may be any that keep to these rules, and one draw needn't show every extreme that they name: `send_counts`: entry 4 p + d is the number of leading live slots in row 4 p + d of send_rows; some entry equals 384. `col_block`: entry k = 0 of row t is t mod (8), the tile's own block; the 4 entries of a row are distinct. `send_rows`: rows of the sending partition; repeats possible. `recv_target`: rows of the receiving partition; repeats possible.
All inputs are finite; a program needn't handle non-finite values.
Results may differ from the reference program's by a relative error of at most 0.008.
Values may be sent and summed in bfloat16 or wider, within the bound.
No kernel may reach another device: no remote copies, remote signals or barrier semaphores. Data moves between devices by JAX's collectives and lax.ppermute only.
A program may use at most 64 MiB of HBM per device.

```python
import jax
import jax.numpy as jnp
from jax import lax

D = 1024
H = 1024
C = 128
NODES = 1024
TB = 128
KT = 4
S = 384
PARTITIONS = 64
NODES_ALL = 65536
BLOCKS_ALL = 512
N_GX = 16
N_GY = 4


def draw_col_block(key, part):
    blocks = NODES // TB
    column_ids = jnp.arange(blocks, dtype=jnp.int32)
    scores = jax.random.randint(key, (BLOCKS_ALL, blocks), 0, 1 << 20, dtype=jnp.int32) * blocks + column_ids[None, :]
    own_block = jnp.arange(BLOCKS_ALL, dtype=jnp.int32) % blocks
    scores = jnp.where(column_ids[None, :] == own_block[:, None], -1, scores)
    ranking = jnp.argsort(scores, axis=1, stable=True)
    return ranking[:, :KT].astype(jnp.int32)


def draw_send_counts(key, part):
    count_key, pick_key = jax.random.split(key)
    counts = jax.random.randint(count_key, (4 * PARTITIONS,), max(1, S // 4), S + 1, dtype=jnp.int32)
    chosen = jax.random.randint(pick_key, (), 0, 4 * PARTITIONS, dtype=jnp.int32)
    return jnp.where(jnp.arange(4 * PARTITIONS, dtype=jnp.int32) == chosen, S, counts).astype(jnp.int32)


def set_ends(drawn, stream_key, smallest, top_value):
    index_at = [jax.random.randint(jax.random.fold_in(stream_key, axis), (), 0, length) for axis, length in enumerate(drawn.shape)]
    widest = drawn.shape.index(max(drawn.shape))
    beside = index_at[:widest] + [(index_at[widest] + 1) % drawn.shape[widest]] + index_at[widest + 1:]
    return drawn.at[tuple(index_at)].set(smallest).at[tuple(beside)].set(top_value)


def levels(own_key, shape, pieces, smallest, top_value):
    loudness = 1.0
    for dim, blocks in pieces:
        draws = jax.random.uniform(jax.random.fold_in(jax.random.fold_in(own_key, 6), dim), (blocks,), jnp.float32, smallest / len(pieces), top_value / len(pieces))
        loudness = loudness * jnp.repeat(jnp.exp(draws), shape[dim] // blocks).reshape((-1,) + (1,) * (len(shape) - 1 - dim))
    return loudness


def scatter_about(stream_key, extent, scale, bound, pieces=(), held_as=jnp.bfloat16):
    result = jax.random.normal(stream_key, extent, jnp.float32) * scale
    if len(pieces) > 0:
        result = levels(stream_key, extent, pieces, -0.22, 0.18) * result
    return jnp.clip(result, min=-bound, max=bound).astype(held_as)


def setup_inputs(seed: int = 0) -> dict:
    key_list = jax.random.split(jax.random.key(seed), 11)
    features = scatter_about(key_list[0], (NODES_ALL, D), 1.0, 6.0, ((0, 64), (1, 4)))
    adj_tiles = scatter_about(key_list[1], (BLOCKS_ALL, KT, TB, TB), (KT * TB) ** -0.5, 0.25, ((0, 64),))
    col_block = draw_col_block(jax.random.fold_in(key_list[10], 71), 0)
    send_rows = set_ends(jax.random.randint(key_list[3], (4 * PARTITIONS, S), 0, NODES), jax.random.fold_in(key_list[3], 1), 0, NODES - 1).astype(jnp.int32)
    send_counts = draw_send_counts(jax.random.fold_in(key_list[10], 71), 0)
    recv_target = set_ends(jax.random.randint(key_list[5], (4 * PARTITIONS, S), 0, NODES), jax.random.fold_in(key_list[5], 1), 0, NODES - 1).astype(jnp.int32)
    edge_weight = scatter_about(key_list[6], (4 * PARTITIONS, S), 1.0, 3.0, ((0, 64),), jnp.float32)
    labels = set_ends(jax.random.randint(key_list[7], (NODES_ALL,), 0, C), jax.random.fold_in(key_list[7], 1), 0, C - 1).astype(jnp.int32)
    w_hidden = scatter_about(key_list[8], (D, H), D ** -0.5, 0.1875, ((0, 4),))
    w_classes = scatter_about(key_list[9], (H, C), (H // 9) ** -0.5, 0.5, ((0, 4),))
    return {"features": features, "adj_tiles": adj_tiles, "col_block": col_block, "send_rows": send_rows, "send_counts": send_counts, "recv_target": recv_target, "edge_weight": edge_weight, "labels": labels, "w_hidden": w_hidden, "w_classes": w_classes}


def aggregate(node_field, adj_tiles, col_block, send_rows, send_counts, recv_target, edge_weight):
    feat_width = node_field.shape[1]
    blocks = NODES // TB
    parts_count = N_GX * N_GY
    local_field = node_field.reshape(parts_count, blocks, TB, feat_width)
    tile_view = adj_tiles.reshape(parts_count, blocks, KT, TB, TB)
    index_view = col_block.reshape(parts_count, blocks, KT)

    def one_part(operands):
        part_field, part_tiles, part_index = operands
        picked = part_field[part_index]
        summed = jnp.einsum("bkij,bkjf->bif", part_tiles.astype(jnp.float32), picked.astype(jnp.float32))
        return summed.reshape(NODES, feat_width)

    local_sum = lax.map(one_part, (local_field, tile_view, index_view)).reshape(parts_count * NODES, feat_width)
    slot_ids = jnp.arange(S, dtype=jnp.int32)
    slot_live = slot_ids[None, :] < send_counts[:, None]
    part_base = (jnp.arange(4 * parts_count, dtype=jnp.int32) // 4) * NODES
    outgoing = node_field[part_base[:, None] + send_rows]
    outgoing = jnp.where(slot_live[:, :, None], outgoing, jnp.zeros((), node_field.dtype))
    grid_out = outgoing.reshape(N_GX, N_GY, 4, S, feat_width)
    zero_row = jnp.zeros_like(grid_out[:1, :, 0])
    zero_col = jnp.zeros_like(grid_out[:, :1, 0])
    from_lower_x = jnp.concatenate([zero_row, grid_out[:-1, :, 0]], 0)
    from_upper_x = jnp.concatenate([grid_out[1:, :, 1], zero_row], 0)
    from_lower_y = jnp.concatenate([zero_col, grid_out[:, :-1, 2]], 1)
    from_upper_y = jnp.concatenate([grid_out[:, 1:, 3], zero_col], 1)
    arrived = jnp.stack([from_lower_x, from_upper_x, from_lower_y, from_upper_y], 2)
    arrived = arrived.reshape(4 * parts_count, S, feat_width)
    weighted = edge_weight[:, :, None] * arrived.astype(jnp.float32)
    targets = part_base[:, None] + recv_target
    return local_sum.at[targets.reshape(-1)].add(weighted.reshape(-1, feat_width))


def aggregate_back(grad_field, adj_tiles, col_block, send_rows, send_counts, recv_target, edge_weight):
    feat_width = grad_field.shape[1]
    blocks = NODES // TB
    parts_count = N_GX * N_GY
    local_grad = grad_field.reshape(parts_count, blocks, TB, feat_width)
    tile_view = adj_tiles.reshape(parts_count, blocks, KT, TB, TB)
    index_view = col_block.reshape(parts_count, blocks, KT)

    def one_part(operands):
        part_grad, part_tiles, part_index = operands
        spread = jnp.einsum("bkij,bif->bkjf", part_tiles.astype(jnp.float32), part_grad.astype(jnp.float32))
        placed = jnp.zeros((blocks, TB, feat_width), jnp.float32)
        placed = placed.at[part_index.reshape(-1)].add(spread.reshape(blocks * KT, TB, feat_width))
        return placed.reshape(NODES, feat_width)

    local_sum = lax.map(one_part, (local_grad, tile_view, index_view)).reshape(parts_count * NODES, feat_width)
    slot_ids = jnp.arange(S, dtype=jnp.int32)
    slot_live = slot_ids[None, :] < send_counts[:, None]
    part_base = (jnp.arange(4 * parts_count, dtype=jnp.int32) // 4) * NODES
    gathered = grad_field[part_base[:, None] + recv_target].astype(jnp.float32)
    back_terms = (edge_weight[:, :, None] * gathered).astype(jnp.bfloat16)
    grid_back = back_terms.reshape(N_GX, N_GY, 4, S, feat_width)
    zero_row = jnp.zeros_like(grid_back[:1, :, 0])
    zero_col = jnp.zeros_like(grid_back[:, :1, 0])
    return_zero = jnp.concatenate([grid_back[1:, :, 0], zero_row], 0)
    return_one = jnp.concatenate([zero_row, grid_back[:-1, :, 1]], 0)
    return_two = jnp.concatenate([grid_back[:, 1:, 2], zero_col], 1)
    return_three = jnp.concatenate([zero_col, grid_back[:, :-1, 3]], 1)
    returned = jnp.stack([return_zero, return_one, return_two, return_three], 2)
    returned = returned.reshape(4 * parts_count, S, feat_width).astype(jnp.float32)
    returned = jnp.where(slot_live[:, :, None], returned, jnp.zeros((), jnp.float32))
    sources = part_base[:, None] + send_rows
    return local_sum.at[sources.reshape(-1)].add(returned.reshape(-1, feat_width))


def reference(features, adj_tiles, col_block, send_rows, send_counts, recv_target, edge_weight, labels, w_hidden, w_classes):
    graph_parts = (adj_tiles, col_block, send_rows, send_counts, recv_target, edge_weight)
    mixed_in = aggregate(features, *graph_parts).astype(jnp.bfloat16)
    pre_act = jnp.dot(mixed_in, w_hidden, preferred_element_type=jnp.float32)
    hidden = jax.nn.silu(pre_act).astype(jnp.bfloat16)
    mixed_hidden = aggregate(hidden, *graph_parts).astype(jnp.bfloat16)
    logits = jnp.dot(mixed_hidden, w_classes, preferred_element_type=jnp.float32)
    exponent = jnp.exp(logits - jnp.max(logits, axis=1, keepdims=True))
    probability = exponent / jnp.sum(exponent, axis=1, keepdims=True)
    onehot = (labels[:, None] == jnp.arange(C, dtype=jnp.int32)[None, :]).astype(jnp.float32)
    grad_logits = ((probability - onehot) / 64.0).astype(jnp.bfloat16)
    grad_classes = jnp.dot(mixed_hidden.T, grad_logits, preferred_element_type=jnp.float32)
    grad_mixed = jnp.dot(grad_logits, w_classes.T, preferred_element_type=jnp.float32).astype(jnp.bfloat16)
    grad_act = aggregate_back(grad_mixed, *graph_parts)
    sigmoid_act = jax.nn.sigmoid(pre_act)
    grad_pre = (grad_act * sigmoid_act * (1.0 + pre_act * (1.0 - sigmoid_act))).astype(jnp.bfloat16)
    grad_hidden = jnp.dot(mixed_in.T, grad_pre, preferred_element_type=jnp.float32)
    return (grad_hidden, grad_classes)
```

```python
import jax
import jax.numpy as jnp
import numpy as np
from jax import lax
from jax.sharding import Mesh
from jax.sharding import PartitionSpec as P

BF = jnp.bfloat16
F32 = jnp.float32
ROWS = ("z", "core")
PLANE = ("z", "gy")


def dot(lhs, rhs, lhs_dim=1, rhs_dim=0):
    return lax.dot_general(lhs, rhs, (((lhs_dim,), (rhs_dim,)), ((), ())), preferred_element_type=F32)


def step(field, axis, move):
    count = lax.axis_size(axis)
    pairs = [(i, i + move) for i in range(count) if 0 <= i + move < count]
    return lax.ppermute(field, axis, pairs)


def turn(field, axis, move):
    count = lax.axis_size(axis)
    return lax.ppermute(field, axis, [(i, (i + move) % count) for i in range(count)])


def trade(fields, sign):
    return jnp.concatenate(
        [
            step(fields[0], ROWS, sign),
            step(fields[1], ROWS, -sign),
            step(fields[2], "gy", sign),
            step(fields[3], "gy", -sign),
        ],
        axis=0,
    )


def two_parts(values):
    high = values.astype(BF)
    low = (values - high.astype(F32)).astype(BF)
    return jnp.concatenate([high, low], axis=1)


def local(
    features,
    adj_tiles,
    col_block,
    send_rows,
    send_counts,
    recv_target,
    edge_weight,
    labels,
    w_hidden,
    w_classes,
):
    af = lax.axis_index("af")
    core = lax.axis_index("core")
    n_af = lax.axis_size("af")
    n_plane = lax.axis_size("z") * lax.axis_size("gy")
    nodes = features.shape[0]
    own = nodes // n_af
    slots = send_rows.shape[1]
    hid = w_hidden.shape[1]
    classes = w_classes.shape[1]
    w_rows = w_hidden.shape[0]
    half = w_rows // 2
    blocks, kt, tb, _ = adj_tiles.shape

    w_both = jnp.concatenate([w_hidden, w_classes], axis=1)
    w_from = [w_both] + [turn(w_both, "af", k) for k in range(1, n_af)]

    live = jnp.arange(slots, dtype=jnp.int32)[None, :] < send_counts[:, None]
    send_at = jnp.where(live, send_rows, -1).reshape(-1)
    recv_at = recv_target.reshape(-1)
    weight = edge_weight.reshape(-1, 1)
    node_ids = jnp.arange(nodes, dtype=jnp.int32)
    pick_send = (send_at[:, None] == node_ids[None, :]).astype(BF)
    pick_recv = (recv_at[:, None] == node_ids[None, :]).astype(BF)
    put_recv = (node_ids[:, None] == recv_at[None, :]).astype(BF)
    own_ids = node_ids[:own] + af * own
    put_send = (own_ids[:, None] == send_at[None, :]).astype(BF)

    block_ids = jnp.arange(blocks, dtype=jnp.int32)
    dense = jnp.zeros((blocks, tb, blocks, tb), BF)
    for k in range(kt):
        here = col_block[:, k][:, None, None, None] == block_ids[None, None, :, None]
        dense = jnp.where(here, adj_tiles[:, k][:, :, None, :], dense)
    dense = dense.reshape(nodes, nodes)

    out = dot(pick_send, features).astype(BF).reshape(4, slots, -1)
    arrived = trade(out, 1).astype(F32) * weight
    width = features.shape[1]
    spread = dot(put_recv, two_parts(arrived))
    mixed = (dot(dense, features) + spread[:, :width] + spread[:, width:]).astype(BF)

    def rows_for(k):
        return lax.dynamic_slice_in_dim(mixed, ((af + k) % n_af) * own, own, axis=0)

    mixed_from = [rows_for(0)] + [turn(rows_for(k), "af", k) for k in range(1, n_af)]
    pre_act = sum(dot(m, w[:, :hid]) for m, w in zip(mixed_from, w_from))
    sigmoid_act = jax.nn.sigmoid(pre_act)
    hidden = (pre_act * sigmoid_act).astype(BF)
    slope = sigmoid_act * (1.0 + pre_act * (1.0 - sigmoid_act))

    w_cls = [w[:, hid:] for w in w_from]
    around = [w_cls[(n_af - k) % n_af] for k in range(n_af)]
    w_cls = lax.dynamic_slice_in_dim(
        jnp.concatenate(around + around, axis=0), (n_af - af) * w_rows, n_af * w_rows, axis=0
    )

    z_own = dot(hidden, w_cls).astype(BF)
    z_all = lax.all_to_all(
        jnp.broadcast_to(z_own[None], (n_af, own, classes)), "af", 0, 0, tiled=True
    ).reshape(nodes, classes)
    out = dot(pick_send, z_all).astype(BF).reshape(4, slots, -1)
    arrived = trade(out, 1).astype(F32) * weight
    spread = dot(put_recv, two_parts(arrived))
    logits = dot(dense, z_all) + spread[:, :classes] + spread[:, classes:]

    exponent = jnp.exp(logits - jnp.max(logits, axis=1, keepdims=True))
    probability = exponent / jnp.sum(exponent, axis=1, keepdims=True)
    onehot = (labels[:, None] == jnp.arange(classes, dtype=jnp.int32)[None, :]).astype(F32)
    grad_logits = ((probability - onehot) / 64.0).astype(BF)

    back = (dot(pick_recv, grad_logits) * weight).astype(BF).reshape(4, slots, -1)
    returned = trade(back, -1)
    dense_own = lax.dynamic_slice_in_dim(dense, af * own, own, axis=1)
    grad_own = (dot(dense_own, grad_logits, 0, 0) + dot(put_send, returned)).astype(BF)
    grad_pre = (dot(grad_own, w_cls, 1, 1) * slope).astype(BF)

    def columns(which):
        return jnp.concatenate(
            [lax.dynamic_slice_in_dim(m, which * half, half, axis=1) for m in mixed_from], axis=1
        )

    def hidden_columns(which):
        return jnp.concatenate(
            [
                lax.dynamic_slice_in_dim(
                    hidden, ((af - k) % n_af) * w_rows + which * half, half, axis=1
                )
                for k in range(n_af)
            ],
            axis=1,
        )

    def terms(which):
        return jnp.concatenate(
            [dot(columns(which), grad_pre, 0, 0), dot(hidden_columns(which), grad_own, 0, 0)],
            axis=1,
        )

    theirs = lax.ppermute(terms(1 - core).astype(BF), "core", [(0, 1), (1, 0)])
    pair_sum = (terms(core) + theirs.astype(F32)).reshape(n_af, half, hid + classes)
    total = pair_sum[0]
    for k in range(1, n_af):
        total = total + turn(pair_sum[k].astype(BF), "af", -k).astype(F32)
    pieces = total.astype(BF).reshape(n_plane, half // n_plane, hid + classes)
    pieces = lax.all_to_all(pieces, PLANE, 0, 0, tiled=True)
    piece = jnp.sum(pieces.astype(F32), axis=0).astype(BF)
    mine = lax.all_to_all(
        jnp.broadcast_to(piece[None], (n_plane,) + piece.shape), PLANE, 0, 0, tiled=True
    ).reshape(half, hid + classes)
    other = lax.ppermute(mine, "core", [(0, 1), (1, 0)])
    first = jnp.where(core == 0, mine, other)
    second = jnp.where(core == 0, other, mine)
    whole = jnp.concatenate([first, second], axis=0).astype(F32)
    return (whole[:, :hid], whole[:, hid:])


def solution(mesh):
    shape = mesh.devices.shape
    split = Mesh(
        np.reshape(mesh.devices, (shape[0] // 2, 2) + shape[1:]), ("z", "core", "gy", "af")
    )
    parts = ("z", "core", "gy")
    placed = (
        P(parts, "af"),
        P(parts, None, None, None),
        P(parts, None),
        P(parts, None),
        P(parts),
        P(parts, None),
        P(parts, None),
        P(parts),
        P("af", None),
        P("af", None),
    )
    return jax.shard_map(
        local, mesh=split, in_specs=placed, out_specs=(P("af", None), P("af", None)), check_vma=False
    )
```

```python
import jax
import jax.numpy as jnp
import numpy as np
from jax import lax
from jax.sharding import Mesh
from jax.sharding import PartitionSpec as P

BF = jnp.bfloat16
F32 = jnp.float32
ROWS = ("z", "core")
PLANE = ("z", "gy")


def dot(lhs, rhs, lhs_dim=1, rhs_dim=0):
    return lax.dot_general(lhs, rhs, (((lhs_dim,), (rhs_dim,)), ((), ())), preferred_element_type=F32)


def step(field, axis, move):
    count = lax.axis_size(axis)
    pairs = [(i, i + move) for i in range(count) if 0 <= i + move < count]
    return lax.ppermute(field, axis, pairs)


def turn(field, axis, move):
    count = lax.axis_size(axis)
    return lax.ppermute(field, axis, [(i, (i + move) % count) for i in range(count)])


def trade(fields, sign):
    return jnp.concatenate(
        [
            step(fields[0], ROWS, sign),
            step(fields[1], ROWS, -sign),
            step(fields[2], "gy", sign),
            step(fields[3], "gy", -sign),
        ],
        axis=0,
    )


def two_parts(values):
    high = values.astype(BF)
    low = (values - high.astype(F32)).astype(BF)
    return jnp.concatenate([high, low], axis=1)


def local(
    features,
    adj_tiles,
    col_block,
    send_rows,
    send_counts,
    recv_target,
    edge_weight,
    labels,
    w_hidden,
    w_classes,
):
    af = lax.axis_index("af")
    core = lax.axis_index("core")
    n_af = lax.axis_size("af")
    n_plane = lax.axis_size("z") * lax.axis_size("gy")
    nodes = features.shape[0]
    own = nodes // n_af
    slots = send_rows.shape[1]
    hid = w_hidden.shape[1]
    classes = w_classes.shape[1]
    w_rows = w_hidden.shape[0]
    half = w_rows // 2
    blocks, kt, tb, _ = adj_tiles.shape

    swap = [(0, 1), (1, 0)]
    w_both = [
        jnp.concatenate(
            [
                lax.dynamic_slice_in_dim(w_hidden, part * half, half, axis=0),
                lax.dynamic_slice_in_dim(w_classes, part * half, half, axis=0),
            ],
            axis=1,
        )
        for part in (core, 1 - core)
    ]
    w_mine = [w_both[0]] + [turn(w_both[0], "af", k) for k in range(1, n_af)]
    w_other = [w_both[1]] + [lax.ppermute(w, "core", swap) for w in w_mine[1:]]

    live = jnp.arange(slots, dtype=jnp.int32)[None, :] < send_counts[:, None]
    send_at = jnp.where(live, send_rows, -1).reshape(-1)
    recv_at = recv_target.reshape(-1)
    weight = edge_weight.reshape(-1, 1)
    node_ids = jnp.arange(nodes, dtype=jnp.int32)
    pick_send = (send_at[:, None] == node_ids[None, :]).astype(BF)
    pick_recv = (recv_at[:, None] == node_ids[None, :]).astype(BF)
    put_recv = (node_ids[:, None] == recv_at[None, :]).astype(BF)
    own_ids = node_ids[:own] + af * own
    put_send = (own_ids[:, None] == send_at[None, :]).astype(BF)

    block_ids = jnp.arange(blocks, dtype=jnp.int32)
    dense = jnp.zeros((blocks, tb, blocks, tb), BF)
    for k in range(kt):
        here = col_block[:, k][:, None, None, None] == block_ids[None, None, :, None]
        dense = jnp.where(here, adj_tiles[:, k][:, :, None, :], dense)
    dense = dense.reshape(nodes, nodes)

    out = dot(pick_send, features).astype(BF).reshape(4, slots, -1)
    arrived = trade(out, 1).astype(F32) * weight
    width = features.shape[1]
    spread = dot(put_recv, two_parts(arrived))
    mixed = (dot(dense, features) + spread[:, :width] + spread[:, width:]).astype(BF)
    mixed = jnp.where(core == 0, mixed, jnp.roll(mixed, half, axis=1))

    def rows_for(k):
        return lax.dynamic_slice_in_dim(mixed, ((af + k) % n_af) * own, own, axis=0)

    mixed_from = [rows_for(0)] + [turn(rows_for(k), "af", k) for k in range(1, n_af)]
    pre_act = sum(
        dot(m[:, :half], w[:, :hid]) + dot(m[:, half:], v[:, :hid])
        for m, w, v in zip(mixed_from, w_mine, w_other)
    )
    sigmoid_act = jax.nn.sigmoid(pre_act)
    hidden = (pre_act * sigmoid_act).astype(BF)
    slope = sigmoid_act * (1.0 + pre_act * (1.0 - sigmoid_act))

    w_cls = []
    for w, v in zip(w_mine, w_other):
        w, v = w[:, hid:], v[:, hid:]
        w_cls.append(jnp.where(core == 0, jnp.concatenate([w, v]), jnp.concatenate([v, w])))
    around = [w_cls[(n_af - k) % n_af] for k in range(n_af)]
    w_cls = lax.dynamic_slice_in_dim(
        jnp.concatenate(around + around, axis=0), (n_af - af) * w_rows, n_af * w_rows, axis=0
    )

    z_own = two_parts(dot(hidden, w_cls))
    z_all = lax.all_to_all(
        jnp.broadcast_to(z_own[None], (n_af,) + z_own.shape), "af", 0, 0, tiled=True
    ).reshape(nodes, 2 * classes)
    out = dot(pick_send, z_all).astype(BF).reshape(4, slots, -1)
    arrived = trade(out, 1).astype(F32)
    arrived = (arrived[:, :classes] + arrived[:, classes:]) * weight
    spread = dot(put_recv, two_parts(arrived)) + dot(dense, z_all)
    logits = spread[:, :classes] + spread[:, classes:]

    exponent = jnp.exp(logits - jnp.max(logits, axis=1, keepdims=True))
    probability = exponent / jnp.sum(exponent, axis=1, keepdims=True)
    onehot = (labels[:, None] == jnp.arange(classes, dtype=jnp.int32)[None, :]).astype(F32)
    grad_logits = ((probability - onehot) / 64.0).astype(BF)

    back = (dot(pick_recv, grad_logits) * weight).astype(BF).reshape(4, slots, -1)
    returned = trade(back, -1)
    dense_own = lax.dynamic_slice_in_dim(dense, af * own, own, axis=1)
    grad_own = (dot(dense_own, grad_logits, 0, 0) + dot(put_send, returned)).astype(BF)
    grad_pre = (dot(grad_own, w_cls, 1, 1) * slope).astype(BF)

    def columns(start):
        return jnp.concatenate([m[:, start : start + half] for m in mixed_from], axis=1)

    def hidden_columns(which):
        return jnp.concatenate(
            [
                lax.dynamic_slice_in_dim(
                    hidden, ((af - k) % n_af) * w_rows + which * half, half, axis=1
                )
                for k in range(n_af)
            ],
            axis=1,
        )

    def terms(start, which):
        return jnp.concatenate(
            [dot(columns(start), grad_pre, 0, 0), dot(hidden_columns(which), grad_own, 0, 0)],
            axis=1,
        )

    theirs = lax.ppermute(terms(half, 1 - core).astype(BF), "core", swap)
    pair_sum = (terms(0, core) + theirs.astype(F32)).reshape(n_af, half, hid + classes)
    total = pair_sum[0]
    for k in range(1, n_af):
        total = total + turn(pair_sum[k].astype(BF), "af", -k).astype(F32)
    pieces = total.astype(BF).reshape(n_plane, half // n_plane, hid + classes)
    pieces = lax.all_to_all(pieces, PLANE, 0, 0, tiled=True)
    piece = jnp.sum(pieces.astype(F32), axis=0).astype(BF)
    mine = lax.all_to_all(
        jnp.broadcast_to(piece[None], (n_plane,) + piece.shape), PLANE, 0, 0, tiled=True
    ).reshape(half, hid + classes)
    other = lax.ppermute(mine, "core", swap)
    first = jnp.where(core == 0, mine, other)
    second = jnp.where(core == 0, other, mine)
    whole = jnp.concatenate([first, second], axis=0).astype(F32)
    return (whole[:, :hid], whole[:, hid:])


def solution(mesh):
    shape = mesh.devices.shape
    split = Mesh(
        np.reshape(mesh.devices, (shape[0] // 2, 2) + shape[1:]), ("z", "core", "gy", "af")
    )
    parts = ("z", "core", "gy")
    placed = (
        P(parts, "af"),
        P(parts, None, None, None),
        P(parts, None),
        P(parts, None),
        P(parts),
        P(parts, None),
        P(parts, None),
        P(parts),
        P("af", None),
        P("af", None),
    )
    return jax.shard_map(
        local, mesh=split, in_specs=placed, out_specs=(P("af", None), P("af", None)), check_vma=False
    )
```

```python
import jax
import jax.numpy as jnp
import numpy as np
from jax import lax
from jax.sharding import Mesh
from jax.sharding import PartitionSpec as P

BF = jnp.bfloat16
F32 = jnp.float32
ROWS = ("z", "core")
PLANE = ("z", "gy")


def dot(lhs, rhs, lhs_dim=1, rhs_dim=0):
    return lax.dot_general(lhs, rhs, (((lhs_dim,), (rhs_dim,)), ((), ())), preferred_element_type=F32)


def step(field, axis, move):
    count = lax.axis_size(axis)
    pairs = [(i, i + move) for i in range(count) if 0 <= i + move < count]
    return lax.ppermute(field, axis, pairs)


def turn(field, axis, move):
    count = lax.axis_size(axis)
    return lax.ppermute(field, axis, [(i, (i + move) % count) for i in range(count)])


def trade(fields, sign):
    return jnp.concatenate(
        [
            step(fields[0], ROWS, sign),
            step(fields[1], ROWS, -sign),
            step(fields[2], "gy", sign),
            step(fields[3], "gy", -sign),
        ],
        axis=0,
    )


def two_parts(values):
    high = lax.reduce_precision(values, 8, 7)
    return jnp.concatenate([high.astype(BF), (values - high).astype(BF)], axis=1)


def local(
    features,
    adj_tiles,
    col_block,
    send_rows,
    send_counts,
    recv_target,
    edge_weight,
    labels,
    w_hidden,
    w_classes,
):
    af = lax.axis_index("af")
    core = lax.axis_index("core")
    n_af = lax.axis_size("af")
    n_plane = lax.axis_size("z") * lax.axis_size("gy")
    nodes = features.shape[0]
    slots = send_rows.shape[1]
    hid = w_hidden.shape[1]
    classes = w_classes.shape[1]
    w_rows = w_hidden.shape[0]
    half = w_rows // 2
    blocks, kt, tb, _ = adj_tiles.shape

    swap = [(0, 1), (1, 0)]
    w_both = [
        jnp.concatenate(
            [
                lax.dynamic_slice_in_dim(w_hidden, part * half, half, axis=0),
                lax.dynamic_slice_in_dim(w_classes, part * half, half, axis=0),
            ],
            axis=1,
        )
        for part in (core, 1 - core)
    ]
    w_mine = [w_both[0]] + [turn(w_both[0], "af", k) for k in range(1, n_af)]
    w_other = [w_both[1]] + [lax.ppermute(w, "core", swap) for w in w_mine[1:]]

    live = jnp.arange(slots, dtype=jnp.int32)[None, :] < send_counts[:, None]
    send_at = jnp.where(live, send_rows, -1).reshape(-1)
    recv_at = recv_target.reshape(-1)
    weight = edge_weight.reshape(-1, 1)
    node_ids = jnp.arange(nodes, dtype=jnp.int32)
    pick_send = (send_at[:, None] == node_ids[None, :]).astype(BF)
    pick_recv = (recv_at[:, None] == node_ids[None, :]).astype(BF)
    put_recv = (node_ids[:, None] == recv_at[None, :]).astype(BF)
    put_send = (node_ids[:, None] == send_at[None, :]).astype(BF)

    block_ids = jnp.arange(blocks, dtype=jnp.int32)
    dense = jnp.zeros((blocks, tb, blocks, tb), BF)
    for k in range(kt):
        here = col_block[:, k][:, None, None, None] == block_ids[None, None, :, None]
        dense = jnp.where(here, adj_tiles[:, k][:, :, None, :], dense)
    dense = dense.reshape(nodes, nodes)

    out = dot(pick_send, features).astype(BF).reshape(4, slots, -1)
    arrived = trade(out, 1).astype(F32) * weight
    width = features.shape[1]
    spread = dot(put_recv, two_parts(arrived))
    mixed = (dot(dense, features) + spread[:, :width] + spread[:, width:]).astype(BF)
    mixed = jnp.where(core == 0, mixed, jnp.roll(mixed, half, axis=1))

    top = nodes // 2
    below = turn(mixed, "af", 1)
    above = turn(mixed, "af", -1)
    across = [turn(below[:top], "af", 1), turn(above[top:], "af", -1)]

    def product(rows, k):
        return dot(rows[:, :half], w_mine[k][:, :hid]) + dot(rows[:, half:], w_other[k][:, :hid])

    pre_act = product(mixed, 0) + product(below, 1) + product(above, 3)
    pre_act = pre_act + jnp.concatenate([product(rows, 2) for rows in across], axis=0)
    sigmoid_act = jax.nn.sigmoid(pre_act)
    hidden = (pre_act * sigmoid_act).astype(BF)
    slope = sigmoid_act * (1.0 + pre_act * (1.0 - sigmoid_act))

    w_cls = []
    for w, v in zip(w_mine, w_other):
        w, v = w[:, hid:], v[:, hid:]
        w_cls.append(jnp.where(core == 0, jnp.concatenate([w, v]), jnp.concatenate([v, w])))
    around = [w_cls[(n_af - k) % n_af] for k in range(n_af)]
    w_cls = lax.dynamic_slice_in_dim(
        jnp.concatenate(around + around, axis=0), (n_af - af) * w_rows, n_af * w_rows, axis=0
    )

    z_pair = two_parts(dot(hidden, w_cls))
    out = dot(pick_send, z_pair[:, :classes]).astype(BF).reshape(4, slots, -1)
    arrived = trade(out, 1).astype(F32) * weight
    spread = dot(put_recv, two_parts(arrived)) + dot(dense, z_pair)
    logits = spread[:, :classes] + spread[:, classes:]

    exponent = jnp.exp(logits - jnp.max(logits, axis=1, keepdims=True))
    probability = exponent / jnp.sum(exponent, axis=1, keepdims=True)
    onehot = (labels[:, None] == jnp.arange(classes, dtype=jnp.int32)[None, :]).astype(F32)
    grad_logits = ((probability - onehot) / 64.0).astype(BF)

    back = (dot(pick_recv, grad_logits) * weight).astype(BF).reshape(4, slots, -1)
    returned = trade(back, -1)
    grad_mix = (dot(dense, grad_logits, 0, 0) + dot(put_send, returned)).astype(BF)
    grad_pre = (dot(grad_mix, w_cls, 1, 1) * slope).astype(BF)

    def terms(start, which):
        units = lax.dynamic_slice_in_dim(hidden, af * w_rows + which * half, half, axis=1)
        return jnp.concatenate(
            [dot(mixed[:, start : start + half], grad_pre, 0, 0), dot(units, grad_mix, 0, 0)],
            axis=1,
        )

    theirs = lax.ppermute(terms(half, 1 - core).astype(BF), "core", swap)
    total = terms(0, core) + theirs.astype(F32)
    pieces = total.astype(BF).reshape(n_plane, half // n_plane, hid + classes)
    pieces = lax.all_to_all(pieces, PLANE, 0, 0, tiled=True)
    piece = jnp.sum(pieces.astype(F32), axis=0).astype(BF)
    mine = lax.all_to_all(
        jnp.broadcast_to(piece[None], (n_plane,) + piece.shape), PLANE, 0, 0, tiled=True
    ).reshape(half, hid + classes)
    other = lax.ppermute(mine, "core", swap)
    first = jnp.where(core == 0, mine, other)
    second = jnp.where(core == 0, other, mine)
    whole = jnp.concatenate([first, second], axis=0).astype(F32)
    return (whole[:, :hid], whole[:, hid:])


def solution(mesh):
    shape = mesh.devices.shape
    split = Mesh(
        np.reshape(mesh.devices, (shape[0] // 2, 2) + shape[1:]), ("z", "core", "gy", "af")
    )
    parts = ("z", "core", "gy")
    placed = (
        P(parts, "af"),
        P(parts, None, None, None),
        P(parts, None),
        P(parts, None),
        P(parts),
        P(parts, None),
        P(parts, None),
        P(parts),
        P("af", None),
        P("af", None),
    )
    return jax.shard_map(
        local, mesh=split, in_specs=placed, out_specs=(P("af", None), P("af", None)), check_vma=False
    )
```

```python
import jax
import jax.numpy as jnp
import numpy as np
from jax import lax
from jax.experimental import pallas as pl
from jax.experimental.pallas import tpu as pltpu
from jax.sharding import Mesh
from jax.sharding import PartitionSpec as P

BF = jnp.bfloat16
F32 = jnp.float32
ROWS = ("z", "core")
PLANE = ("z", "gy")
LANES = 128
INTERPRET = False


def dot(lhs, rhs, lhs_dim=1, rhs_dim=0):
    return lax.dot_general(lhs, rhs, (((lhs_dim,), (rhs_dim,)), ((), ())), preferred_element_type=F32)


def turn(field, axis, move):
    count = lax.axis_size(axis)
    return lax.ppermute(field, axis, [(i, (i + move) % count) for i in range(count)])


def pairs_at(count, first):
    pairs = []
    for i in range(first, count - 1, 2):
        pairs += [(i, i + 1), (i + 1, i)]
    return pairs


def trade(fields):
    rows, cols = lax.axis_size(ROWS), lax.axis_size("gy")
    return (
        lax.ppermute(fields[0], "core", [(0, 1), (1, 0)]),
        lax.ppermute(fields[1], ROWS, pairs_at(rows, 1)),
        lax.ppermute(fields[2], "gy", pairs_at(cols, 0)),
        lax.ppermute(fields[3], "gy", pairs_at(cols, 1)),
    )


def send_order(meta):
    core, odd = meta[0], lax.rem(meta[1], 2)
    return (core, 1 - core, 2 + odd, 3 - odd)


def recv_order(meta):
    core, odd = meta[0], lax.rem(meta[1], 2)
    return (1 - core, core, 3 - odd, 2 + odd)


def down(row):
    return jnp.transpose(jnp.broadcast_to(row.astype(F32), (LANES, LANES)))


def pick(row, nodes, out_ref):
    lane = lax.broadcasted_iota(jnp.int32, (LANES, LANES), 1).astype(F32)
    for b in range(row.shape[1] // LANES):
        at = down(row[:, b * LANES : (b + 1) * LANES])
        for j in range(nodes // LANES):
            out_ref[b * LANES : (b + 1) * LANES, j * LANES : (j + 1) * LANES] = jnp.where(
                at == lane + float(j * LANES), 1.0, 0.0
            ).astype(BF)


def put(row, nodes):
    ids = lax.broadcasted_iota(jnp.int32, (nodes, row.shape[1]), 0)
    return jnp.where(ids == row, 1.0, 0.0).astype(BF)


def live_row(send_ref, counts, d):
    row = send_ref[pl.ds(d, 1), :]
    slot = lax.broadcasted_iota(jnp.int32, row.shape, 1)
    return jnp.where(slot < counts[d], row, -1)


def weigh(arrived, weight_row, rhs_ref, base):
    width = arrived.shape[1]
    for b in range(weight_row.shape[1] // LANES):
        w = down(weight_row[:, b * LANES : (b + 1) * LANES])
        w = jnp.concatenate([w] * (width // LANES), axis=1)
        value = arrived[b * LANES : (b + 1) * LANES, :].astype(F32) * w
        high = value.astype(BF)
        low = (value - high.astype(F32)).astype(BF)
        rhs_ref[pl.ds(base + b * LANES, LANES), :width] = high
        rhs_ref[pl.ds(base + b * LANES, LANES), width:] = low


def send_kernel(meta, counts, feat, send, w_hid, w_cls, o0, o1, o2, o3, mine, other, hot):
    nodes = feat.shape[0]
    half, hid = w_hid.shape[0] // 2, w_hid.shape[1]
    for ref, part in ((mine, meta[0]), (other, 1 - meta[0])):
        at = pl.multiple_of(part * half, half)
        ref[:, :hid] = w_hid[pl.ds(at, half), :]
        ref[:, hid:] = w_cls[pl.ds(at, half), :]
    for d, out in zip(send_order(meta), (o0, o1, o2, o3)):
        pick(live_row(send, counts, d), nodes, hot)
        out[...] = dot(hot[...], feat[...]).astype(BF)


def near(tiles, col, field, block, tb):
    lhs = jnp.concatenate([tiles[block, k] for k in range(tiles.shape[1])], axis=1)
    rhs = jnp.concatenate(
        [
            field[pl.ds(pl.multiple_of(col[block, k] * tb, tb), tb), :]
            for k in range(tiles.shape[1])
        ],
        axis=0,
    )
    return dot(lhs, rhs)


def mix_kernel(meta, col, feat, tiles, r0, r1, r2, r3, recv, weight, top, bottom, hot, rhs):
    nodes, width = feat.shape
    slots, tb = recv.shape[1], tiles.shape[2]
    for m, (d, arrived) in enumerate(zip(recv_order(meta), (r0, r1, r2, r3))):
        hot[:, m * slots : (m + 1) * slots] = put(recv[pl.ds(d, 1), :], nodes)
        weigh(arrived[...], weight[pl.ds(d, 1), :], rhs, m * slots)
    part = nodes // 2
    first = meta[0] == 0
    for h, out in enumerate((top, bottom)):
        far = dot(hot[h * part : (h + 1) * part, :], rhs[...])
        far = far[:, :width] + far[:, width:]
        for b in range(part // tb):
            got = near(tiles, col, feat, h * (part // tb) + b, tb) + far[b * tb : (b + 1) * tb, :]
            turned = jnp.concatenate([got[:, width // 2 :], got[:, : width // 2]], axis=1)
            out[b * tb : (b + 1) * tb, :] = jnp.where(first, got, turned).astype(BF)


def hidden_kernel(
    meta, counts, send, own_t, own_b, lo_t, lo_b, hi_t, hi_b, far_t, far_b,
    m0, m1, m2, m3, v0, v1, v2, v3,
    hidden, slope, z_pair, w_cls, o0, o1, o2, o3, w_all, hot,
):
    nodes = z_pair.shape[0]
    half = m0.shape[0]
    hid = w_all.shape[1]
    classes = w_cls.shape[1]
    n_af = w_cls.shape[0] // (2 * half)
    for i, (k, mine, other) in enumerate(((0, m0, v0), (1, m1, v1), (3, m3, v3), (2, m2, v2))):
        w_all[2 * i * half : (2 * i + 1) * half, :] = mine[:, :hid]
        w_all[(2 * i + 1) * half : (2 * i + 2) * half, :] = other[:, :hid]
        base = lax.rem(meta[2] + n_af - k, n_af) * 2
        w_cls[pl.ds(pl.multiple_of((base + meta[0]) * half, half), half), :] = mine[:, hid:]
        w_cls[pl.ds(pl.multiple_of((base + 1 - meta[0]) * half, half), half), :] = other[:, hid:]
    part = nodes // 2
    rows = 256
    for h, refs in enumerate(((own_t, lo_t, hi_t, far_t), (own_b, lo_b, hi_b, far_b))):

        def block(i, carry, h=h, refs=refs):
            at = pl.multiple_of(i * rows, rows)
            to = pl.multiple_of(h * part + i * rows, rows)
            lhs = jnp.concatenate([ref[pl.ds(at, rows), :] for ref in refs], axis=1)
            pre = dot(lhs, w_all[...])
            sig = jax.nn.sigmoid(pre)
            act = (pre * sig).astype(BF)
            slope[pl.ds(to, rows), :] = (sig * (1.0 + pre * (1.0 - sig))).astype(BF)
            for j in range(hid // LANES):
                hidden[j, pl.ds(to, rows), :] = act[:, j * LANES : (j + 1) * LANES]
            z = dot(act, w_cls[...])
            high = z.astype(BF)
            z_pair[pl.ds(to, rows), :classes] = high
            z_pair[pl.ds(to, rows), classes:] = (z - high.astype(F32)).astype(BF)
            return carry

        lax.fori_loop(0, part // rows, block, 0)
    for d, out in zip(send_order(meta), (o0, o1, o2, o3)):
        pick(live_row(send, counts, d), nodes, hot)
        out[...] = dot(hot[...], z_pair[:, :classes]).astype(BF)


def loss_kernel(
    meta, col, tiles, z_pair, r0, r1, r2, r3, recv, weight, labels,
    grad, b0, b1, b2, b3, hot, rhs, cols,
):
    nodes, classes = grad.shape
    slots, tb = recv.shape[1], tiles.shape[2]
    order = recv_order(meta)
    for m, (d, arrived) in enumerate(zip(order, (r0, r1, r2, r3))):
        hot[:, m * slots : (m + 1) * slots] = put(recv[pl.ds(d, 1), :], nodes)
        weigh(arrived[...], weight[pl.ds(d, 1), :], rhs, m * slots)
    part = nodes // 2
    lane = lax.broadcasted_iota(jnp.int32, (tb, classes), 1).astype(F32)
    for h in range(2):
        far = dot(hot[h * part : (h + 1) * part, :], rhs[...])
        for b in range(part // tb):
            r = h * (part // tb) + b
            logit = near(tiles, col, z_pair, r, tb) + far[b * tb : (b + 1) * tb, :]
            logit = logit[:, :classes] + logit[:, classes:]
            exponent = jnp.exp(logit - jnp.max(logit, axis=1, keepdims=True))
            probability = exponent / jnp.sum(exponent, axis=1, keepdims=True)
            onehot = jnp.where(down(labels[r : r + 1, :]) == lane, 1.0, 0.0)
            grad[r * tb : (r + 1) * tb, :] = ((probability - onehot) * (1.0 / 64.0)).astype(BF)
    for d, out in zip(order, (b0, b1, b2, b3)):
        pick(recv[pl.ds(d, 1), :], nodes, cols)
        taken = dot(cols[...], grad[...])
        row = weight[pl.ds(d, 1), :]
        for b in range(slots // LANES):
            at = slice(b * LANES, (b + 1) * LANES)
            out[at, :] = (taken[at, :] * down(row[:, at])).astype(BF)


def grads_kernel(
    meta, col, counts, pick_hid, tiles, grad, t0, t1, t2, t3, send, w_cls, slope, top, bottom,
    units_m, units_o, theirs, mine, hot, back, acc, mix, pre,
):
    nodes, classes = grad.shape
    slots, tb, kt = send.shape[1], tiles.shape[2], tiles.shape[1]
    hid = slope.shape[1]
    for m, (d, returned) in enumerate(zip(send_order(meta), (t0, t1, t2, t3))):
        hot[:, m * slots : (m + 1) * slots] = put(live_row(send, counts, d), nodes)
        back[m * slots : (m + 1) * slots, :] = returned[...]
    acc[...] = dot(hot[...], back[...])
    for r in range(tiles.shape[0]):
        lhs = jnp.concatenate([tiles[r, k] for k in range(kt)], axis=1)
        spread = dot(lhs, grad[r * tb : (r + 1) * tb, :], 0, 0)
        for k in range(kt):
            at = pl.ds(pl.multiple_of(col[r, k] * tb, tb), tb)
            acc[at, :] += spread[k * tb : (k + 1) * tb, :]
    mix[...] = acc[...].astype(BF)
    rows = 256

    def block(i, carry):
        at = pl.ds(pl.multiple_of(i * rows, rows), rows)
        act = dot(mix[at, :], w_cls[...], 1, 1)
        pre[at, :] = (act * slope[at, :].astype(F32)).astype(BF)
        return carry

    lax.fori_loop(0, nodes // rows, block, 0)
    lhs = jnp.concatenate([top[...], bottom[...]], axis=0)
    both = dot(lhs, pre[...], 0, 0)
    half = both.shape[0] // 2
    mine[:, :hid] = both[:half]
    theirs[:, :hid] = both[half:].astype(BF)
    mine[:, hid:] = dot(units_m[0], mix[...], 0, 0)
    theirs[:, hid:] = dot(units_o[0], mix[...], 0, 0).astype(BF)


def call(kernel, scalars, arrays, outs, scratch, specs=None):
    def whole(x):
        return pl.BlockSpec(x.shape, lambda *_, n=len(x.shape): (0,) * n)

    specs = specs or {}
    outs = [jax.ShapeDtypeStruct(s, t) for s, t in outs]
    return pl.pallas_call(
        kernel,
        grid_spec=pltpu.PrefetchScalarGridSpec(
            num_scalar_prefetch=len(scalars),
            grid=(1,),
            in_specs=[specs.get(i, whole(x)) for i, x in enumerate(arrays)],
            out_specs=[whole(x) for x in outs],
            scratch_shapes=[pltpu.VMEM(s, t) for s, t in scratch],
        ),
        out_shape=outs,
        interpret=INTERPRET,
        name=kernel.__name__,
    )(*scalars, *arrays)


def local(
    features,
    adj_tiles,
    col_block,
    send_rows,
    send_counts,
    recv_target,
    edge_weight,
    labels,
    w_hidden,
    w_classes,
):
    nodes, width = features.shape
    slots = send_rows.shape[1]
    hid, classes = w_hidden.shape[1], w_classes.shape[1]
    half = w_hidden.shape[0] // 2
    n_af = lax.axis_size("af")
    n_plane = lax.axis_size("z") * lax.axis_size("gy")
    core = lax.axis_index("core")
    af = lax.axis_index("af")
    meta = jnp.stack([core, lax.axis_index("gy"), af]).astype(jnp.int32)
    swap = [(0, 1), (1, 0)]
    both = hid + classes
    part = nodes // 2

    *out, w_mine, w_other = call(
        send_kernel,
        (meta, send_counts),
        (features, send_rows, w_hidden, w_classes),
        [((slots, width), BF)] * 4 + [((half, both), BF)] * 2,
        [((slots, nodes), BF)],
    )
    arrived = trade(out)
    w_mine = [w_mine] + [turn(w_mine, "af", k) for k in range(1, n_af)]
    w_other = [w_other] + [lax.ppermute(w, "core", swap) for w in w_mine[1:]]
    top, bottom = call(
        mix_kernel,
        (meta, col_block),
        (features, adj_tiles, *arrived, recv_target, edge_weight),
        [((part, width), BF)] * 2,
        [((nodes, 4 * slots), BF), ((4 * slots, 2 * width), BF)],
    )
    lo_t, hi_b = turn(top, "af", 1), turn(bottom, "af", -1)
    lo_b, hi_t = turn(bottom, "af", 1), turn(top, "af", -1)
    far_t, far_b = turn(lo_t, "af", 1), turn(hi_b, "af", -1)
    hidden, slope, z_pair, w_cls, *out = call(
        hidden_kernel,
        (meta, send_counts),
        (send_rows, top, bottom, lo_t, lo_b, hi_t, hi_b, far_t, far_b, *w_mine, *w_other),
        [
            ((hid // LANES, nodes, LANES), BF),
            ((nodes, hid), BF),
            ((nodes, 2 * classes), BF),
            ((hid, classes), BF),
        ]
        + [((slots, classes), BF)] * 4,
        [((n_af * 2 * half, hid), BF), ((slots, nodes), BF)],
    )
    arrived = trade(out)
    grad, *out = call(
        loss_kernel,
        (meta, col_block),
        (adj_tiles, z_pair, *arrived, recv_target, edge_weight, labels.reshape(-1, LANES)),
        [((nodes, classes), BF)] + [((slots, classes), BF)] * 4,
        [((nodes, 4 * slots), BF), ((4 * slots, 2 * classes), BF), ((slots, nodes), BF)],
    )
    returned = trade(out)
    pick_hid = jnp.stack([af * 2 + core, af * 2 + 1 - core]).astype(jnp.int32)
    theirs, mine = call(
        grads_kernel,
        (meta, col_block, send_counts, pick_hid),
        (adj_tiles, grad, *returned, send_rows, w_cls, slope, top, bottom, hidden, hidden),
        [((half, both), BF), ((half, both), F32)],
        [
            ((nodes, 4 * slots), BF),
            ((4 * slots, classes), BF),
            ((nodes, classes), F32),
            ((nodes, classes), BF),
            ((nodes, hid), BF),
        ],
        {
            11: pl.BlockSpec((1, nodes, LANES), lambda i, a, b, c, s: (s[0], 0, 0)),
            12: pl.BlockSpec((1, nodes, LANES), lambda i, a, b, c, s: (s[1], 0, 0)),
        },
    )
    total = mine + lax.ppermute(theirs, "core", swap).astype(F32)
    pieces = total.astype(BF).reshape(n_plane, half // n_plane, both)
    pieces = lax.all_to_all(pieces, PLANE, 0, 0, tiled=True)
    piece = jnp.sum(pieces.astype(F32), axis=0).astype(BF)
    mine = lax.all_to_all(
        jnp.broadcast_to(piece[None], (n_plane,) + piece.shape), PLANE, 0, 0, tiled=True
    ).reshape(half, both)
    other = lax.ppermute(mine, "core", swap)
    first = jnp.where(core == 0, mine, other)
    second = jnp.where(core == 0, other, mine)
    whole = jnp.concatenate([first, second], axis=0).astype(F32)
    return (whole[:, :hid], whole[:, hid:])


def solution(mesh):
    shape = mesh.devices.shape
    split = Mesh(
        np.reshape(mesh.devices, (shape[0] // 2, 2) + shape[1:]), ("z", "core", "gy", "af")
    )
    parts = ("z", "core", "gy")
    placed = (
        P(parts, "af"),
        P(parts, None, None, None),
        P(parts, None),
        P(parts, None),
        P(parts),
        P(parts, None),
        P(parts, None),
        P(parts),
        P("af", None),
        P("af", None),
    )
    return jax.shard_map(
        local, mesh=split, in_specs=placed, out_specs=(P("af", None), P("af", None)), check_vma=False
    )
```

```python
import jax
import jax.numpy as jnp
import numpy as np
from jax import lax
from jax.experimental import pallas as pl
from jax.experimental.pallas import tpu as pltpu
from jax.sharding import Mesh
from jax.sharding import PartitionSpec as P

BF = jnp.bfloat16
F32 = jnp.float32
ROWS = ("z", "core")
PLANE = ("z", "gy")
LANES = 128
INTERPRET = False


def dot(lhs, rhs, lhs_dim=1, rhs_dim=0):
    return lax.dot_general(lhs, rhs, (((lhs_dim,), (rhs_dim,)), ((), ())), preferred_element_type=F32)


def turn(field, axis, move):
    count = lax.axis_size(axis)
    return lax.ppermute(field, axis, [(i, (i + move) % count) for i in range(count)])


def pairs_at(count, first):
    pairs = []
    for i in range(first, count - 1, 2):
        pairs += [(i, i + 1), (i + 1, i)]
    return pairs


def trade(fields):
    rows, cols = lax.axis_size(ROWS), lax.axis_size("gy")
    return (
        lax.ppermute(fields[0], "core", [(0, 1), (1, 0)]),
        lax.ppermute(fields[1], ROWS, pairs_at(rows, 1)),
        lax.ppermute(fields[2], "gy", pairs_at(cols, 0)),
        lax.ppermute(fields[3], "gy", pairs_at(cols, 1)),
    )


def send_order(meta):
    core, odd = meta[0], lax.rem(meta[1], 2)
    return (core, 1 - core, 2 + odd, 3 - odd)


def recv_order(meta):
    core, odd = meta[0], lax.rem(meta[1], 2)
    return (1 - core, core, 3 - odd, 2 + odd)


def down(row):
    return jnp.transpose(jnp.broadcast_to(row.astype(F32), (LANES, LANES)))


def pick(row, nodes, out_ref):
    lane = lax.broadcasted_iota(jnp.int32, (LANES, LANES), 1).astype(F32)
    for b in range(row.shape[1] // LANES):
        at = down(row[:, b * LANES : (b + 1) * LANES])
        for j in range(nodes // LANES):
            out_ref[b * LANES : (b + 1) * LANES, j * LANES : (j + 1) * LANES] = jnp.where(
                at == lane + float(j * LANES), 1.0, 0.0
            ).astype(BF)


def put(row, nodes):
    ids = lax.broadcasted_iota(jnp.int32, (nodes, row.shape[1]), 0)
    return jnp.where(ids == row, 1.0, 0.0).astype(BF)


def live_row(send_ref, counts, d):
    row = send_ref[pl.ds(d, 1), :]
    slot = lax.broadcasted_iota(jnp.int32, row.shape, 1)
    return jnp.where(slot < counts[d], row, -1)


def weigh(arrived, weight_row, rhs_ref, base):
    width = arrived.shape[1]
    for b in range(weight_row.shape[1] // LANES):
        w = down(weight_row[:, b * LANES : (b + 1) * LANES])
        w = jnp.concatenate([w] * (width // LANES), axis=1)
        value = arrived[b * LANES : (b + 1) * LANES, :].astype(F32) * w
        high = value.astype(BF)
        low = (value - high.astype(F32)).astype(BF)
        rhs_ref[pl.ds(base + b * LANES, LANES), :width] = high
        rhs_ref[pl.ds(base + b * LANES, LANES), width:] = low


def send_kernel(meta, counts, feat, send, w_hid, w_cls, o0, o1, o2, o3, mine, other, hot):
    nodes = feat.shape[0]
    half, hid = w_hid.shape[0] // 2, w_hid.shape[1]
    for ref, part in ((mine, meta[0]), (other, 1 - meta[0])):
        at = pl.multiple_of(part * half, half)
        ref[:, :hid] = w_hid[pl.ds(at, half), :]
        ref[:, hid:] = w_cls[pl.ds(at, half), :]
    for d, out in zip(send_order(meta), (o0, o1, o2, o3)):
        pick(live_row(send, counts, d), nodes, hot)
        out[...] = dot(hot[...], feat[...]).astype(BF)


def near(tiles, col, field, block, tb):
    lhs = jnp.concatenate([tiles[block, k] for k in range(tiles.shape[1])], axis=1)
    rhs = jnp.concatenate(
        [
            field[pl.ds(pl.multiple_of(col[block, k] * tb, tb), tb), :]
            for k in range(tiles.shape[1])
        ],
        axis=0,
    )
    return dot(lhs, rhs)


def mix_kernel(meta, col, feat, tiles, r0, r1, r2, r3, recv, weight, top, bottom, hot, rhs):
    nodes, width = feat.shape
    slots, tb = recv.shape[1], tiles.shape[2]
    for m, (d, arrived) in enumerate(zip(recv_order(meta), (r0, r1, r2, r3))):
        hot[:, m * slots : (m + 1) * slots] = put(recv[pl.ds(d, 1), :], nodes)
        weigh(arrived[...], weight[pl.ds(d, 1), :], rhs, m * slots)
    part = nodes // 2
    first = meta[0] == 0
    for h, out in enumerate((top, bottom)):
        far = dot(hot[h * part : (h + 1) * part, :], rhs[...])
        far = far[:, :width] + far[:, width:]
        for b in range(part // tb):
            got = near(tiles, col, feat, h * (part // tb) + b, tb) + far[b * tb : (b + 1) * tb, :]
            turned = jnp.concatenate([got[:, width // 2 :], got[:, : width // 2]], axis=1)
            out[b * tb : (b + 1) * tb, :] = jnp.where(first, got, turned).astype(BF)


def hidden_kernel(
    meta, counts, send, own_t, own_b, lo_t, lo_b, hi_t, hi_b, far_t, far_b,
    m0, m1, m2, m3, v0, v1, v2, v3,
    hidden, slope, z_pair, w_cls, o0, o1, o2, o3, w_all, hot,
):
    nodes = z_pair.shape[0]
    half = m0.shape[0]
    hid = w_all.shape[1]
    classes = w_cls.shape[1]
    n_af = w_cls.shape[0] // (2 * half)
    for i, (k, mine, other) in enumerate(((0, m0, v0), (1, m1, v1), (3, m3, v3), (2, m2, v2))):
        w_all[2 * i * half : (2 * i + 1) * half, :] = mine[:, :hid]
        w_all[(2 * i + 1) * half : (2 * i + 2) * half, :] = other[:, :hid]
        base = lax.rem(meta[2] + n_af - k, n_af) * 2
        w_cls[pl.ds(pl.multiple_of((base + meta[0]) * half, half), half), :] = mine[:, hid:]
        w_cls[pl.ds(pl.multiple_of((base + 1 - meta[0]) * half, half), half), :] = other[:, hid:]
    part = nodes // 2
    rows = 256
    for h, refs in enumerate(((own_t, lo_t, hi_t, far_t), (own_b, lo_b, hi_b, far_b))):

        def block(i, carry, h=h, refs=refs):
            at = pl.multiple_of(i * rows, rows)
            to = pl.multiple_of(h * part + i * rows, rows)
            lhs = jnp.concatenate([ref[pl.ds(at, rows), :] for ref in refs], axis=1)
            pre = dot(lhs, w_all[...])
            sig = jax.nn.sigmoid(pre)
            act = (pre * sig).astype(BF)
            slope[pl.ds(to, rows), :] = (sig * (1.0 + pre * (1.0 - sig))).astype(BF)
            for j in range(hid // LANES):
                hidden[j, pl.ds(to, rows), :] = act[:, j * LANES : (j + 1) * LANES]
            z = dot(act, w_cls[...])
            high = z.astype(BF)
            z_pair[pl.ds(to, rows), :classes] = high
            z_pair[pl.ds(to, rows), classes:] = (z - high.astype(F32)).astype(BF)
            return carry

        lax.fori_loop(0, part // rows, block, 0)
    for d, out in zip(send_order(meta), (o0, o1, o2, o3)):
        pick(live_row(send, counts, d), nodes, hot)
        out[...] = dot(hot[...], z_pair[:, :classes]).astype(BF)


def loss_kernel(
    meta, col, tiles, z_pair, r0, r1, r2, r3, recv, weight, labels,
    grad, b0, b1, b2, b3, hot, rhs, cols,
):
    nodes, classes = grad.shape
    slots, tb = recv.shape[1], tiles.shape[2]
    order = recv_order(meta)
    for m, (d, arrived) in enumerate(zip(order, (r0, r1, r2, r3))):
        hot[:, m * slots : (m + 1) * slots] = put(recv[pl.ds(d, 1), :], nodes)
        weigh(arrived[...], weight[pl.ds(d, 1), :], rhs, m * slots)
    part = nodes // 2
    lane = lax.broadcasted_iota(jnp.int32, (tb, classes), 1).astype(F32)
    for h in range(2):
        far = dot(hot[h * part : (h + 1) * part, :], rhs[...])
        for b in range(part // tb):
            r = h * (part // tb) + b
            logit = near(tiles, col, z_pair, r, tb) + far[b * tb : (b + 1) * tb, :]
            logit = logit[:, :classes] + logit[:, classes:]
            exponent = jnp.exp(logit - jnp.max(logit, axis=1, keepdims=True))
            probability = exponent / jnp.sum(exponent, axis=1, keepdims=True)
            onehot = jnp.where(down(labels[r : r + 1, :]) == lane, 1.0, 0.0)
            grad[r * tb : (r + 1) * tb, :] = ((probability - onehot) * (1.0 / 64.0)).astype(BF)
    for d, out in zip(order, (b0, b1, b2, b3)):
        pick(recv[pl.ds(d, 1), :], nodes, cols)
        taken = dot(cols[...], grad[...])
        row = weight[pl.ds(d, 1), :]
        for b in range(slots // LANES):
            at = slice(b * LANES, (b + 1) * LANES)
            out[at, :] = (taken[at, :] * down(row[:, at])).astype(BF)


def grads_kernel(
    meta, col, counts, tiles, grad, t0, t1, t2, t3, send, w_cls, slope, top, bottom,
    units_m, units_o, theirs, mine, hot, back, acc, mix, pre,
):
    nodes, _ = grad.shape
    slots, tb, kt = send.shape[1], tiles.shape[2], tiles.shape[1]
    hid = slope.shape[1]
    for m, (d, returned) in enumerate(zip(send_order(meta), (t0, t1, t2, t3))):
        hot[:, m * slots : (m + 1) * slots] = put(live_row(send, counts, d), nodes)
        back[m * slots : (m + 1) * slots, :] = returned[...]
    acc[...] = dot(hot[...], back[...])
    for r in range(tiles.shape[0]):
        lhs = jnp.concatenate([tiles[r, k] for k in range(kt)], axis=1)
        spread = dot(lhs, grad[r * tb : (r + 1) * tb, :], 0, 0)
        for k in range(kt):
            at = pl.ds(pl.multiple_of(col[r, k] * tb, tb), tb)
            acc[at, :] += spread[k * tb : (k + 1) * tb, :]
    mix[...] = acc[...].astype(BF)
    rows = 256

    def block(i, carry):
        at = pl.ds(pl.multiple_of(i * rows, rows), rows)
        act = dot(mix[at, :], w_cls[...], 1, 1)
        pre[at, :] = (act * slope[at, :].astype(F32)).astype(BF)
        return carry

    lax.fori_loop(0, nodes // rows, block, 0)
    lhs = jnp.concatenate([top[...], bottom[...]], axis=0)
    both = dot(lhs, pre[...], 0, 0)
    half = both.shape[0] // 2
    mine[:, :hid] = both[:half]
    theirs[:, :hid] = both[half:].astype(BF)
    mine[:, hid:] = dot(units_m[0], mix[...], 0, 0)
    theirs[:, hid:] = dot(units_o[0], mix[...], 0, 0).astype(BF)


def join_kernel(meta, mine, other, grad_hidden, grad_classes):
    half, hid = mine.shape[0], grad_hidden.shape[1]
    for ref, part in ((mine, meta[0]), (other, 1 - meta[0])):
        at = pl.ds(pl.multiple_of(part * half, half), half)
        grad_hidden[at, :] = ref[:, :hid].astype(F32)
        grad_classes[at, :] = ref[:, hid:].astype(F32)


def call(kernel, scalars, arrays, outs, scratch, specs=None):
    def whole(x):
        return pl.BlockSpec(x.shape, lambda *_, n=len(x.shape): (0,) * n)

    specs = specs or {}
    outs = [jax.ShapeDtypeStruct(s, t) for s, t in outs]
    return pl.pallas_call(
        kernel,
        grid_spec=pltpu.PrefetchScalarGridSpec(
            num_scalar_prefetch=len(scalars),
            grid=(1,),
            in_specs=[specs.get(i, whole(x)) for i, x in enumerate(arrays)],
            out_specs=[whole(x) for x in outs],
            scratch_shapes=[pltpu.VMEM(s, t) for s, t in scratch],
        ),
        out_shape=outs,
        interpret=INTERPRET,
    )(*scalars, *arrays)


def work(
    features,
    adj_tiles,
    col_block,
    send_rows,
    send_counts,
    recv_target,
    edge_weight,
    labels,
    w_hidden,
    w_classes,
):
    nodes, width = features.shape
    slots = send_rows.shape[1]
    hid, classes = w_hidden.shape[1], w_classes.shape[1]
    half = w_hidden.shape[0] // 2
    n_af = lax.axis_size("af")
    n_plane = lax.axis_size("z") * lax.axis_size("gy")
    core = lax.axis_index("core")
    af = lax.axis_index("af")
    meta = jnp.stack([core, lax.axis_index("gy"), af]).astype(jnp.int32)
    swap = [(0, 1), (1, 0)]
    both = hid + classes
    part = nodes // 2

    *out, w_mine, w_other = call(
        send_kernel,
        (meta, send_counts),
        (features, send_rows, w_hidden, w_classes),
        [((slots, width), BF)] * 4 + [((half, both), BF)] * 2,
        [((slots, nodes), BF)],
    )
    arrived = trade(out)
    w_mine = [w_mine] + [turn(w_mine, "af", k) for k in range(1, n_af)]
    w_other = [w_other] + [lax.ppermute(w_mine[k], "core", swap) for k in range(1, n_af)]
    top, bottom = call(
        mix_kernel,
        (meta, col_block),
        (features, adj_tiles, *arrived, recv_target, edge_weight),
        [((part, width), BF)] * 2,
        [((nodes, 4 * slots), BF), ((4 * slots, 2 * width), BF)],
    )
    lo_t, hi_b = turn(top, "af", 1), turn(bottom, "af", -1)
    lo_b, hi_t = turn(bottom, "af", 1), turn(top, "af", -1)
    far_t, far_b = turn(lo_t, "af", 1), turn(hi_b, "af", -1)
    hidden, slope, z_pair, w_cls, *out = call(
        hidden_kernel,
        (meta, send_counts),
        (send_rows, top, bottom, lo_t, lo_b, hi_t, hi_b, far_t, far_b, *w_mine, *w_other),
        [
            ((hid // LANES, nodes, LANES), BF),
            ((nodes, hid), BF),
            ((nodes, 2 * classes), BF),
            ((hid, classes), BF),
        ]
        + [((slots, classes), BF)] * 4,
        [((n_af * 2 * half, hid), BF), ((slots, nodes), BF)],
    )
    arrived = trade(out)
    grad, *out = call(
        loss_kernel,
        (meta, col_block),
        (adj_tiles, z_pair, *arrived, recv_target, edge_weight, labels.reshape(-1, LANES)),
        [((nodes, classes), BF)] + [((slots, classes), BF)] * 4,
        [((nodes, 4 * slots), BF), ((4 * slots, 2 * classes), BF), ((slots, nodes), BF)],
    )
    returned = trade(out)
    theirs, mine = call(
        grads_kernel,
        (meta, col_block, send_counts),
        (adj_tiles, grad, *returned, send_rows, w_cls, slope, top, bottom, hidden, hidden),
        [((half, both), BF), ((half, both), F32)],
        [
            ((nodes, 4 * slots), BF),
            ((4 * slots, classes), BF),
            ((nodes, classes), F32),
            ((nodes, classes), BF),
            ((nodes, hid), BF),
        ],
        {
            11: pl.BlockSpec((1, nodes, LANES), lambda i, m, c, n: (m[2] * 2 + m[0], 0, 0)),
            12: pl.BlockSpec((1, nodes, LANES), lambda i, m, c, n: (m[2] * 2 + 1 - m[0], 0, 0)),
        },
    )
    total = mine + lax.ppermute(theirs, "core", swap).astype(F32)
    pieces = total.astype(BF).reshape(n_plane, half // n_plane, both)
    pieces = lax.all_to_all(pieces, PLANE, 0, 0, tiled=True)
    piece = jnp.sum(pieces.astype(F32), axis=0).astype(BF)
    mine = lax.all_to_all(
        jnp.broadcast_to(piece[None], (n_plane,) + piece.shape), PLANE, 0, 0, tiled=True
    ).reshape(half, both)
    other = lax.ppermute(mine, "core", swap)
    grad_hidden, grad_classes = call(
        join_kernel,
        (meta,),
        (mine, other),
        [((2 * half, hid), F32), ((2 * half, classes), F32)],
        [],
    )
    return (grad_hidden, grad_classes)


def solution(mesh):
    shape = mesh.devices.shape
    split = Mesh(
        np.reshape(mesh.devices, (shape[0] // 2, 2) + shape[1:]), ("z", "core", "gy", "af")
    )
    parts = ("z", "core", "gy")
    placed = (
        P(parts, "af"),
        P(parts, None, None, None),
        P(parts, None),
        P(parts, None),
        P(parts),
        P(parts, None),
        P(parts, None),
        P(parts),
        P("af", None),
        P("af", None),
    )
    return jax.shard_map(
        work,
        mesh=split,
        in_specs=placed,
        out_specs=(P("af", None), P("af", None)),
        check_vma=False,
    )
```

```python
import jax
import jax.numpy as jnp
import numpy as np
from jax import lax
from jax.experimental import pallas as pl
from jax.experimental.pallas import tpu as pltpu
from jax.sharding import Mesh
from jax.sharding import PartitionSpec as P

BF = jnp.bfloat16
F32 = jnp.float32
ROWS = ("z", "core")
PLANE = ("z", "gy")
LANES = 128
INTERPRET = False


def dot(lhs, rhs, lhs_dim=1, rhs_dim=0):
    return lax.dot_general(lhs, rhs, (((lhs_dim,), (rhs_dim,)), ((), ())), preferred_element_type=F32)


def turn(field, axis, move):
    count = lax.axis_size(axis)
    return lax.ppermute(field, axis, [(i, (i + move) % count) for i in range(count)])


def pairs_at(count, first):
    pairs = []
    for i in range(first, count - 1, 2):
        pairs += [(i, i + 1), (i + 1, i)]
    return pairs


def trade(fields):
    rows, cols = lax.axis_size(ROWS), lax.axis_size("gy")
    return (
        lax.ppermute(fields[0], "core", [(0, 1), (1, 0)]),
        lax.ppermute(fields[1], ROWS, pairs_at(rows, 1)),
        lax.ppermute(fields[2], "gy", pairs_at(cols, 0)),
        lax.ppermute(fields[3], "gy", pairs_at(cols, 1)),
    )


def send_order(meta):
    core, odd = meta[0], lax.rem(meta[1], 2)
    return (core, 1 - core, 2 + odd, 3 - odd)


def recv_order(meta):
    core, odd = meta[0], lax.rem(meta[1], 2)
    return (1 - core, core, 3 - odd, 2 + odd)


def down(row):
    return jnp.transpose(jnp.broadcast_to(row.astype(F32), (LANES, LANES)))


def halves(row):
    high = jnp.floor(row.astype(F32) * (1.0 / LANES))
    return high, row.astype(F32) - high * LANES


def pick(row, nodes, out_ref):
    lane = lax.broadcasted_iota(jnp.int32, (LANES, LANES), 1).astype(F32)
    high, low = halves(row)
    none = jnp.zeros((LANES, LANES), BF)
    for b in range(row.shape[1] // LANES):
        at = slice(b * LANES, (b + 1) * LANES)
        match = jnp.where(down(low[:, at]) == lane, 1.0, 0.0).astype(BF)
        block = down(high[:, at]).astype(BF)
        for j in range(nodes // LANES):
            out_ref[at, j * LANES : (j + 1) * LANES] = jnp.where(
                block == jnp.asarray(j, BF), match, none
            )


def put(row, nodes, out_ref, base):
    slots = row.shape[1]
    high, low = halves(row)
    ids = lax.broadcasted_iota(jnp.int32, (LANES, slots), 0).astype(F32)
    match = jnp.where(low == ids, 1.0, 0.0).astype(BF)
    block = jnp.broadcast_to(high, (LANES, slots)).astype(BF)
    none = jnp.zeros((LANES, slots), BF)
    for j in range(nodes // LANES):
        out_ref[j * LANES : (j + 1) * LANES, base : base + slots] = jnp.where(
            block == jnp.asarray(j, BF), match, none
        )


def live_row(send_ref, counts, d):
    row = send_ref[pl.ds(d, 1), :]
    slot = lax.broadcasted_iota(jnp.int32, row.shape, 1)
    return jnp.where(slot < counts[d], row, -1)


def weigh(arrived, weight_row, rhs_ref, base):
    width = arrived.shape[1]
    for b in range(weight_row.shape[1] // LANES):
        w = down(weight_row[:, b * LANES : (b + 1) * LANES])
        w = jnp.concatenate([w] * (width // LANES), axis=1)
        value = arrived[b * LANES : (b + 1) * LANES, :].astype(F32) * w
        high = value.astype(BF)
        low = (value - high.astype(F32)).astype(BF)
        rhs_ref[pl.ds(base + b * LANES, LANES), :width] = high
        rhs_ref[pl.ds(base + b * LANES, LANES), width:] = low


class Mover:
    def __init__(self, sems):
        self.sems, self.used, self.left = sems, 0, []

    def start(self, source, target):
        copy = pltpu.make_async_copy(source, target, self.sems.at[self.used])
        self.used += 1
        copy.start()
        self.left.append(copy)
        return copy

    def wait(self, *copies):
        for copy in copies:
            if any(copy is other for other in self.left):
                self.left = [other for other in self.left if other is not copy]
                copy.wait()

    def finish(self):
        self.wait(*list(self.left))


def send_kernel(
    meta, counts, feat_in, send_in, w_hid, w_cls, o0, o1, o2, o3, mine, other,
    feat, send, hot, out, sems,
):
    nodes = feat.shape[0]
    half, hid = w_hid.shape[0] // 2, w_hid.shape[1]
    mover = Mover(sems)
    got_send = mover.start(send_in, send)
    got_feat = mover.start(feat_in, feat)
    for ref, part in ((mine, meta[0]), (other, 1 - meta[0])):
        at = pl.ds(pl.multiple_of(part * half, half), half)
        mover.start(w_hid.at[at, :], ref.at[:, :hid])
        mover.start(w_cls.at[at, :], ref.at[:, hid:])
    mover.wait(got_send)
    for m, (d, ref) in enumerate(zip(send_order(meta), (o0, o1, o2, o3))):
        pick(live_row(send, counts, d), nodes, hot)
        mover.wait(got_feat)
        out[m] = dot(hot[...], feat[...]).astype(BF)
        mover.start(out.at[m], ref)
    mover.finish()


def near(tiles, col, field, block, tb):
    lhs = jnp.concatenate([tiles[block, k] for k in range(tiles.shape[1])], axis=1)
    rhs = jnp.concatenate(
        [
            field[pl.ds(pl.multiple_of(col[block, k] * tb, tb), tb), :]
            for k in range(tiles.shape[1])
        ],
        axis=0,
    )
    return dot(lhs, rhs)


def mix_kernel(
    meta, col, feat_in, tiles_in, r0, r1, r2, r3, recv_in, weight_in, top, bottom,
    feat, tiles, come, recv, weight, hot, rhs, base, out, sems,
):
    nodes, width = feat.shape
    slots, tb = recv.shape[1], tiles.shape[2]
    order = recv_order(meta)
    mover = Mover(sems)
    first = [mover.start(recv_in, recv), mover.start(weight_in, weight)]
    second = [mover.start(feat_in, feat), mover.start(tiles_in, tiles)]
    third = [mover.start(ref, come.at[m]) for m, ref in enumerate((r0, r1, r2, r3))]
    mover.wait(*first)
    for m, d in enumerate(order):
        put(recv[pl.ds(d, 1), :], nodes, hot, m * slots)
    mover.wait(*second)
    for r in range(nodes // tb):
        base[r * tb : (r + 1) * tb, :] = near(tiles, col, feat, r, tb)
    for m, d in enumerate(order):
        mover.wait(third[m])
        weigh(come[m], weight[pl.ds(d, 1), :], rhs, m * slots)
    part = nodes // 2
    straight = meta[0] == 0
    for h, ref in enumerate((top, bottom)):
        at = slice(h * part, (h + 1) * part)
        far = dot(hot[at, :], rhs[...])
        got = base[at, :] + far[:, :width] + far[:, width:]
        turned = jnp.concatenate([got[:, width // 2 :], got[:, : width // 2]], axis=1)
        out[at, :] = jnp.where(straight, got, turned).astype(BF)
        mover.start(out.at[at, :], ref)
    mover.finish()


def hidden_kernel(
    meta, counts, send_in, own_t, own_b, lo_t, lo_b, hi_t, hi_b, far_t, far_b,
    m0, m1, m2, m3, v0, v1, v2, v3,
    hidden_out, slope_out, z_out, cls_out, o0, o1, o2, o3,
    send, fields, w_all, w_cls, hidden, slope, z_pair, hot, out, sems,
):
    nodes, classes = z_out.shape[0], cls_out.shape[1]
    half, width = m0.shape[0], own_t.shape[1]
    hid = w_all.shape[1]
    n_af = w_all.shape[0] // (2 * half)
    part = nodes // 2
    mover = Mover(sems)
    first = []
    for i, (k, mine, other) in enumerate(((0, m0, v0), (1, m1, v1), (3, m3, v3), (2, m2, v2))):
        at = lax.rem(meta[2] + n_af - k, n_af) * 2
        for ref, row, to in (
            (mine, 2 * i * half, at + meta[0]),
            (other, (2 * i + 1) * half, at + 1 - meta[0]),
        ):
            to = pl.ds(pl.multiple_of(to * half, half), half)
            first.append(mover.start(ref.at[:, :hid], w_all.at[row : row + half, :]))
            first.append(mover.start(ref.at[:, hid:], w_cls.at[to, :]))
    sides = []
    for h, refs in enumerate(((own_t, lo_t, hi_t, far_t), (own_b, lo_b, hi_b, far_b))):
        rows = slice(h * part, (h + 1) * part)
        sides.append(
            [
                mover.start(ref, fields.at[rows, i * width : (i + 1) * width])
                for i, ref in enumerate(refs)
            ]
        )
    got_send = mover.start(send_in, send)
    mover.wait(*first)
    mover.start(w_cls, cls_out)
    rows = 256

    def block(i, carry):
        at = pl.ds(pl.multiple_of(i * rows, rows), rows)
        pre = dot(fields[at, :], w_all[...])
        sig = jax.nn.sigmoid(pre)
        act = (pre * sig).astype(BF)
        slope[at, :] = (sig * (1.0 + pre * (1.0 - sig))).astype(BF)
        for j in range(hid // LANES):
            hidden[j, at, :] = act[:, j * LANES : (j + 1) * LANES]
        z = dot(act, w_cls[...])
        high = z.astype(BF)
        z_pair[at, :classes] = high
        z_pair[at, classes:] = (z - high.astype(F32)).astype(BF)
        return carry

    for h in range(2):
        mover.wait(*sides[h])
        lax.fori_loop(h * part // rows, (h + 1) * part // rows, block, 0)
        at = slice(h * part, (h + 1) * part)
        mover.start(hidden.at[:, at, :], hidden_out.at[:, at, :])
        mover.start(slope.at[at, :], slope_out.at[at, :])
    mover.start(z_pair, z_out)
    mover.wait(got_send)
    for m, (d, ref) in enumerate(zip(send_order(meta), (o0, o1, o2, o3))):
        pick(live_row(send, counts, d), nodes, hot)
        out[m] = dot(hot[...], z_pair[:, :classes]).astype(BF)
        mover.start(out.at[m], ref)
    mover.finish()


def loss_kernel(
    meta, col, tiles_in, z_in, r0, r1, r2, r3, recv_in, weight_in, labels_in,
    grad_out, b0, b1, b2, b3,
    tiles, z_pair, come, recv, weight, labels, hot, rhs, cols, base, grad, out, sems,
):
    nodes, classes = grad.shape
    slots, tb = recv.shape[1], tiles.shape[2]
    order = recv_order(meta)
    mover = Mover(sems)
    first = [mover.start(recv_in, recv), mover.start(weight_in, weight)]
    second = [mover.start(z_in, z_pair), mover.start(tiles_in, tiles)]
    third = [mover.start(ref, come.at[m]) for m, ref in enumerate((r0, r1, r2, r3))]
    last = mover.start(labels_in, labels)
    mover.wait(*first)
    for m, d in enumerate(order):
        put(recv[pl.ds(d, 1), :], nodes, hot, m * slots)
        pick(recv[pl.ds(d, 1), :], nodes, cols.at[m])
    mover.wait(*second)
    for r in range(nodes // tb):
        got = near(tiles, col, z_pair, r, tb)
        base[r * tb : (r + 1) * tb, :] = got[:, :classes] + got[:, classes:]
    for m, d in enumerate(order):
        mover.wait(third[m])
        weigh(come[m], weight[pl.ds(d, 1), :], rhs, m * slots)
    mover.wait(last)
    lane = lax.broadcasted_iota(jnp.int32, (tb, classes), 1).astype(F32)
    part = nodes // 2
    for h in range(2):
        far = dot(hot[h * part : (h + 1) * part, :], rhs[...])
        for b in range(part // tb):
            r = h * (part // tb) + b
            at = slice(r * tb, (r + 1) * tb)
            logit = far[b * tb : (b + 1) * tb, :]
            logit = base[at, :] + logit[:, :classes] + logit[:, classes:]
            exponent = jnp.exp(logit - jnp.max(logit, axis=1, keepdims=True))
            probability = exponent / jnp.sum(exponent, axis=1, keepdims=True)
            onehot = jnp.where(down(labels[r : r + 1, :]) == lane, 1.0, 0.0)
            grad[at, :] = ((probability - onehot) * (1.0 / 64.0)).astype(BF)
    mover.start(grad, grad_out)
    for m, (d, ref) in enumerate(zip(order, (b0, b1, b2, b3))):
        taken = dot(cols[m], grad[...])
        row = weight[pl.ds(d, 1), :]
        for b in range(slots // LANES):
            at = slice(b * LANES, (b + 1) * LANES)
            out[m, at, :] = (taken[at, :] * down(row[:, at])).astype(BF)
        mover.start(out.at[m], ref)
    mover.finish()


def grads_kernel(
    meta, col, counts, tiles_in, grad_in, t0, t1, t2, t3, send_in, cls_in, slope_in, top, bottom,
    hidden, theirs_out, mine_out,
    tiles, grad, send, w_cls, slope, lhs, units, hot, back, acc, mix, pre, theirs, mine, sems,
):
    nodes, _ = grad.shape
    slots, tb, kt = send.shape[1], tiles.shape[2], tiles.shape[1]
    hid = slope.shape[1]
    part = nodes // 2
    mover = Mover(sems)
    first = mover.start(send_in, send)
    second = [mover.start(grad_in, grad), mover.start(tiles_in, tiles)]
    third = [
        mover.start(ref, back.at[m * slots : (m + 1) * slots, :])
        for m, ref in enumerate((t0, t1, t2, t3))
    ]
    fourth = [mover.start(cls_in, w_cls), mover.start(slope_in, slope)]
    own = meta[2] * 2
    last = [
        mover.start(top, lhs.at[:part, :]),
        mover.start(bottom, lhs.at[part:, :]),
        mover.start(hidden.at[own + meta[0]], units.at[0]),
        mover.start(hidden.at[own + 1 - meta[0]], units.at[1]),
    ]
    mover.wait(first)
    for m, d in enumerate(send_order(meta)):
        put(live_row(send, counts, d), nodes, hot, m * slots)
    mover.wait(*third)
    acc[...] = dot(hot[...], back[...])
    mover.wait(*second)
    for r in range(tiles.shape[0]):
        rows = jnp.concatenate([tiles[r, k] for k in range(kt)], axis=1)
        spread = dot(rows, grad[r * tb : (r + 1) * tb, :], 0, 0)
        for k in range(kt):
            at = pl.ds(pl.multiple_of(col[r, k] * tb, tb), tb)
            acc[at, :] += spread[k * tb : (k + 1) * tb, :]
    mix[...] = acc[...].astype(BF)
    mover.wait(*fourth)
    rows = 256

    def block(i, carry):
        at = pl.ds(pl.multiple_of(i * rows, rows), rows)
        act = dot(mix[at, :], w_cls[...], 1, 1)
        pre[at, :] = (act * slope[at, :].astype(F32)).astype(BF)
        return carry

    lax.fori_loop(0, nodes // rows, block, 0)
    mover.wait(*last)
    half = theirs.shape[0]
    theirs[:, :hid] = dot(lhs[:, half:], pre[...], 0, 0).astype(BF)
    theirs[:, hid:] = dot(units[1], mix[...], 0, 0).astype(BF)
    mover.start(theirs, theirs_out)
    mine[:, :hid] = dot(lhs[:, :half], pre[...], 0, 0)
    mine[:, hid:] = dot(units[0], mix[...], 0, 0)
    mover.start(mine, mine_out)
    mover.finish()


def call(kernel, scalars, arrays, outs, scratch, copies):
    outs = [jax.ShapeDtypeStruct(s, t) for s, t in outs]
    return pl.pallas_call(
        kernel,
        in_specs=[pl.BlockSpec(memory_space=pltpu.SMEM) for _ in scalars]
        + [pl.BlockSpec(memory_space=pl.ANY) for _ in arrays],
        out_specs=[pl.BlockSpec(memory_space=pl.ANY) for _ in outs],
        scratch_shapes=[pltpu.VMEM(s, t) for s, t in scratch]
        + [pltpu.SemaphoreType.DMA((copies,))],
        out_shape=outs,
        interpret=INTERPRET,
    )(*scalars, *arrays)


def work(
    features,
    adj_tiles,
    col_block,
    send_rows,
    send_counts,
    recv_target,
    edge_weight,
    labels,
    w_hidden,
    w_classes,
):
    nodes, width = features.shape
    slots = send_rows.shape[1]
    hid, classes = w_hidden.shape[1], w_classes.shape[1]
    half = w_hidden.shape[0] // 2
    n_af = lax.axis_size("af")
    n_plane = lax.axis_size("z") * lax.axis_size("gy")
    core = lax.axis_index("core")
    af = lax.axis_index("af")
    meta = jnp.stack([core, lax.axis_index("gy"), af]).astype(jnp.int32)
    swap = [(0, 1), (1, 0)]
    both = hid + classes
    part = nodes // 2

    nodes_by = (nodes, 4 * slots)
    index_shape = ((4, slots), jnp.int32)
    weight_shape = ((4, slots), F32)
    tiles_shape = (adj_tiles.shape, BF)
    *out, w_mine, w_other = call(
        send_kernel,
        (meta, send_counts),
        (features, send_rows, w_hidden, w_classes),
        [((slots, width), BF)] * 4 + [((half, both), BF)] * 2,
        [(features.shape, BF), index_shape, ((slots, nodes), BF), ((4, slots, width), BF)],
        10,
    )
    arrived = trade(out)
    w_mine = [w_mine] + [turn(w_mine, "af", k) for k in range(1, n_af)]
    w_other = [w_other] + [
        lax.ppermute(w_mine[k], "core", swap) for k in range(1, n_af)
    ]
    top, bottom = call(
        mix_kernel,
        (meta, col_block),
        (features, adj_tiles, *arrived, recv_target, edge_weight),
        [((part, width), BF)] * 2,
        [
            (features.shape, BF),
            tiles_shape,
            ((4, slots, width), BF),
            index_shape,
            weight_shape,
            (nodes_by, BF),
            ((4 * slots, 2 * width), BF),
            ((nodes, width), F32),
            ((nodes, width), BF),
        ],
        10,
    )
    lo_t, hi_b = turn(top, "af", 1), turn(bottom, "af", -1)
    lo_b, hi_t = turn(bottom, "af", 1), turn(top, "af", -1)
    far_t, far_b = turn(lo_t, "af", 1), turn(hi_b, "af", -1)
    hidden, slope, z_pair, w_cls, *out = call(
        hidden_kernel,
        (meta, send_counts),
        (send_rows, top, bottom, lo_t, lo_b, hi_t, hi_b, far_t, far_b, *w_mine, *w_other),
        [
            ((hid // LANES, nodes, LANES), BF),
            ((nodes, hid), BF),
            ((nodes, 2 * classes), BF),
            ((hid, classes), BF),
        ]
        + [((slots, classes), BF)] * 4,
        [
            index_shape,
            ((nodes, n_af * width), BF),
            ((n_af * 2 * half, hid), BF),
            ((hid, classes), BF),
            ((hid // LANES, nodes, LANES), BF),
            ((nodes, hid), BF),
            ((nodes, 2 * classes), BF),
            ((slots, nodes), BF),
            ((4, slots, classes), BF),
        ],
        35,
    )
    arrived = trade(out)
    grad, *out = call(
        loss_kernel,
        (meta, col_block),
        (adj_tiles, z_pair, *arrived, recv_target, edge_weight, labels.reshape(-1, LANES)),
        [((nodes, classes), BF)] + [((slots, classes), BF)] * 4,
        [
            tiles_shape,
            ((nodes, 2 * classes), BF),
            ((4, slots, classes), BF),
            index_shape,
            weight_shape,
            ((nodes // LANES, LANES), jnp.int32),
            (nodes_by, BF),
            ((4 * slots, 2 * classes), BF),
            ((4, slots, nodes), BF),
            ((nodes, classes), F32),
            ((nodes, classes), BF),
            ((4, slots, classes), BF),
        ],
        14,
    )
    returned = trade(out)
    theirs, mine = call(
        grads_kernel,
        (meta, col_block, send_counts),
        (adj_tiles, grad, *returned, send_rows, w_cls, slope, top, bottom, hidden),
        [((half, both), BF), ((half, both), F32)],
        [
            tiles_shape,
            ((nodes, classes), BF),
            index_shape,
            ((hid, classes), BF),
            ((nodes, hid), BF),
            ((nodes, width), BF),
            ((2, nodes, LANES), BF),
            (nodes_by, BF),
            ((4 * slots, classes), BF),
            ((nodes, classes), F32),
            ((nodes, classes), BF),
            ((nodes, hid), BF),
            ((half, both), BF),
            ((half, both), F32),
        ],
        16,
    )
    total = mine + lax.ppermute(theirs, "core", swap).astype(F32)
    pieces = total.astype(BF).reshape(n_plane, half // n_plane, both)
    pieces = lax.all_to_all(pieces, PLANE, 0, 0, tiled=True)
    piece = jnp.sum(pieces.astype(F32), axis=0).astype(BF)
    mine = lax.all_to_all(
        jnp.broadcast_to(piece[None], (n_plane,) + piece.shape), PLANE, 0, 0, tiled=True
    ).reshape(half, both)
    other = lax.ppermute(mine, "core", swap)
    first = jnp.where(core == 0, mine, other)
    second = jnp.where(core == 0, other, mine)
    return (
        jnp.concatenate([first[:, :hid], second[:, :hid]], axis=0).astype(F32),
        jnp.concatenate([first[:, hid:], second[:, hid:]], axis=0).astype(F32),
    )


def solution(mesh):
    shape = mesh.devices.shape
    split = Mesh(
        np.reshape(mesh.devices, (shape[0] // 2, 2) + shape[1:]), ("z", "core", "gy", "af")
    )
    parts = ("z", "core", "gy")
    placed = (
        P(parts, "af"),
        P(parts, None, None, None),
        P(parts, None),
        P(parts, None),
        P(parts),
        P(parts, None),
        P(parts, None),
        P(parts),
        P("af", None),
        P("af", None),
    )
    return jax.shard_map(
        work,
        mesh=split,
        in_specs=placed,
        out_specs=(P("af", None), P("af", None)),
        check_vma=False,
    )
```

```python
import jax
import jax.numpy as jnp
import numpy as np
from jax import lax
from jax.experimental import pallas as pl
from jax.experimental.pallas import tpu as pltpu
from jax.sharding import Mesh
from jax.sharding import PartitionSpec as P

BF = jnp.bfloat16
F32 = jnp.float32
ROWS = ("z", "core")
PLANE = ("z", "gy")
LANES = 128
INTERPRET = False


def dot(lhs, rhs, lhs_dim=1, rhs_dim=0):
    return lax.dot_general(lhs, rhs, (((lhs_dim,), (rhs_dim,)), ((), ())), preferred_element_type=F32)


def turn(field, axis, move):
    count = lax.axis_size(axis)
    return lax.ppermute(field, axis, [(i, (i + move) % count) for i in range(count)])


def pairs_at(count, first):
    pairs = []
    for i in range(first, count - 1, 2):
        pairs += [(i, i + 1), (i + 1, i)]
    return pairs


def trade(fields):
    rows, cols = lax.axis_size(ROWS), lax.axis_size("gy")
    return (
        lax.ppermute(fields[0], "core", [(0, 1), (1, 0)]),
        lax.ppermute(fields[1], ROWS, pairs_at(rows, 1)),
        lax.ppermute(fields[2], "gy", pairs_at(cols, 0)),
        lax.ppermute(fields[3], "gy", pairs_at(cols, 1)),
    )


def send_order(meta):
    core, odd = meta[0], lax.rem(meta[1], 2)
    return (core, 1 - core, 2 + odd, 3 - odd)


def recv_order(meta):
    core, odd = meta[0], lax.rem(meta[1], 2)
    return (1 - core, core, 3 - odd, 2 + odd)


def down(row):
    return jnp.transpose(jnp.broadcast_to(row.astype(F32), (LANES, LANES)))


def pick(row, nodes, out_ref):
    lane = lax.broadcasted_iota(jnp.int32, (LANES, LANES), 1).astype(F32)
    for b in range(row.shape[1] // LANES):
        at = down(row[:, b * LANES : (b + 1) * LANES])
        for j in range(nodes // LANES):
            out_ref[b * LANES : (b + 1) * LANES, j * LANES : (j + 1) * LANES] = jnp.where(
                at == lane + float(j * LANES), 1.0, 0.0
            ).astype(BF)


def put(row, nodes):
    ids = lax.broadcasted_iota(jnp.int32, (nodes, row.shape[1]), 0)
    return jnp.where(ids == row, 1.0, 0.0).astype(BF)


def live_row(send_ref, counts, d):
    row = send_ref[pl.ds(d, 1), :]
    slot = lax.broadcasted_iota(jnp.int32, row.shape, 1)
    return jnp.where(slot < counts[d], row, -1)


def weigh(arrived, weight_row, rhs_ref, base):
    width = arrived.shape[1]
    for b in range(weight_row.shape[1] // LANES):
        w = down(weight_row[:, b * LANES : (b + 1) * LANES])
        w = jnp.concatenate([w] * (width // LANES), axis=1)
        value = arrived[b * LANES : (b + 1) * LANES, :].astype(F32) * w
        high = value.astype(BF)
        low = (value - high.astype(F32)).astype(BF)
        rhs_ref[pl.ds(base + b * LANES, LANES), :width] = high
        rhs_ref[pl.ds(base + b * LANES, LANES), width:] = low


def send_kernel(meta, counts, feat, send, w_hid, w_cls, o0, o1, o2, o3, mine, other, hot):
    nodes = feat.shape[0]
    half, hid = w_hid.shape[0] // 2, w_hid.shape[1]
    for ref, part in ((mine, meta[0]), (other, 1 - meta[0])):
        at = pl.multiple_of(part * half, half)
        ref[:, :hid] = w_hid[pl.ds(at, half), :]
        ref[:, hid:] = w_cls[pl.ds(at, half), :]
    for d, out in zip(send_order(meta), (o0, o1, o2, o3)):
        pick(live_row(send, counts, d), nodes, hot)
        out[...] = dot(hot[...], feat[...]).astype(BF)


def near(tiles, col, field, block, tb):
    lhs = jnp.concatenate([tiles[block, k] for k in range(tiles.shape[1])], axis=1)
    rhs = jnp.concatenate(
        [
            field[pl.ds(pl.multiple_of(col[block, k] * tb, tb), tb), :]
            for k in range(tiles.shape[1])
        ],
        axis=0,
    )
    return dot(lhs, rhs)


def mix_kernel(meta, col, feat, tiles, r0, r1, r2, r3, recv, weight, top, bottom, hot, rhs):
    nodes, width = feat.shape
    slots, tb = recv.shape[1], tiles.shape[2]
    for m, (d, arrived) in enumerate(zip(recv_order(meta), (r0, r1, r2, r3))):
        hot[:, m * slots : (m + 1) * slots] = put(recv[pl.ds(d, 1), :], nodes)
        weigh(arrived[...], weight[pl.ds(d, 1), :], rhs, m * slots)
    part = nodes // 2
    first = meta[0] == 0
    for h, out in enumerate((top, bottom)):
        far = dot(hot[h * part : (h + 1) * part, :], rhs[...])
        far = far[:, :width] + far[:, width:]
        for b in range(part // tb):
            got = near(tiles, col, feat, h * (part // tb) + b, tb) + far[b * tb : (b + 1) * tb, :]
            turned = jnp.concatenate([got[:, width // 2 :], got[:, : width // 2]], axis=1)
            out[b * tb : (b + 1) * tb, :] = jnp.where(first, got, turned).astype(BF)


def hidden_kernel(
    meta, counts, send, own_t, own_b, lo_t, lo_b, hi_t, hi_b, far_t, far_b,
    m0, m1, m2, m3, v0, v1, v2, v3,
    hidden, slope, z_pair, w_cls, o0, o1, o2, o3, w_all, hot,
):
    nodes = z_pair.shape[0]
    half = m0.shape[0]
    hid = w_all.shape[1]
    classes = w_cls.shape[1]
    n_af = w_cls.shape[0] // (2 * half)
    for i, (k, mine, other) in enumerate(((0, m0, v0), (1, m1, v1), (3, m3, v3), (2, m2, v2))):
        w_all[2 * i * half : (2 * i + 1) * half, :] = mine[:, :hid]
        w_all[(2 * i + 1) * half : (2 * i + 2) * half, :] = other[:, :hid]
        base = lax.rem(meta[2] + n_af - k, n_af) * 2
        w_cls[pl.ds(pl.multiple_of((base + meta[0]) * half, half), half), :] = mine[:, hid:]
        w_cls[pl.ds(pl.multiple_of((base + 1 - meta[0]) * half, half), half), :] = other[:, hid:]
    part = nodes // 2
    rows = 256
    for h, refs in enumerate(((own_t, lo_t, hi_t, far_t), (own_b, lo_b, hi_b, far_b))):

        def block(i, carry, h=h, refs=refs):
            at = pl.multiple_of(i * rows, rows)
            to = pl.multiple_of(h * part + i * rows, rows)
            lhs = jnp.concatenate([ref[pl.ds(at, rows), :] for ref in refs], axis=1)
            pre = dot(lhs, w_all[...])
            sig = jax.nn.sigmoid(pre)
            act = (pre * sig).astype(BF)
            slope[pl.ds(to, rows), :] = (sig * (1.0 + pre * (1.0 - sig))).astype(BF)
            for j in range(hid // LANES):
                hidden[j, pl.ds(to, rows), :] = act[:, j * LANES : (j + 1) * LANES]
            z = dot(act, w_cls[...])
            high = z.astype(BF)
            z_pair[pl.ds(to, rows), :classes] = high
            z_pair[pl.ds(to, rows), classes:] = (z - high.astype(F32)).astype(BF)
            return carry

        lax.fori_loop(0, part // rows, block, 0)
    for d, out in zip(send_order(meta), (o0, o1, o2, o3)):
        pick(live_row(send, counts, d), nodes, hot)
        out[...] = dot(hot[...], z_pair[:, :classes]).astype(BF)


def loss_kernel(
    meta, col, tiles, z_pair, r0, r1, r2, r3, recv, weight, labels,
    grad, b0, b1, b2, b3, hot, rhs, cols,
):
    nodes, classes = grad.shape
    slots, tb = recv.shape[1], tiles.shape[2]
    order = recv_order(meta)
    for m, (d, arrived) in enumerate(zip(order, (r0, r1, r2, r3))):
        hot[:, m * slots : (m + 1) * slots] = put(recv[pl.ds(d, 1), :], nodes)
        weigh(arrived[...], weight[pl.ds(d, 1), :], rhs, m * slots)
    part = nodes // 2
    lane = lax.broadcasted_iota(jnp.int32, (tb, classes), 1).astype(F32)
    for h in range(2):
        far = dot(hot[h * part : (h + 1) * part, :], rhs[...])
        for b in range(part // tb):
            r = h * (part // tb) + b
            logit = near(tiles, col, z_pair, r, tb) + far[b * tb : (b + 1) * tb, :]
            logit = logit[:, :classes] + logit[:, classes:]
            exponent = jnp.exp(logit - jnp.max(logit, axis=1, keepdims=True))
            probability = exponent / jnp.sum(exponent, axis=1, keepdims=True)
            onehot = jnp.where(down(labels[r : r + 1, :]) == lane, 1.0, 0.0)
            grad[r * tb : (r + 1) * tb, :] = ((probability - onehot) * (1.0 / 64.0)).astype(BF)
    for d, out in zip(order, (b0, b1, b2, b3)):
        pick(recv[pl.ds(d, 1), :], nodes, cols)
        taken = dot(cols[...], grad[...])
        row = weight[pl.ds(d, 1), :]
        for b in range(slots // LANES):
            at = slice(b * LANES, (b + 1) * LANES)
            out[at, :] = (taken[at, :] * down(row[:, at])).astype(BF)


def grads_kernel(
    meta, col, counts, tiles, grad, t0, t1, t2, t3, send, w_cls, slope, top, bottom,
    hidden, theirs, mine, hot, back, acc, mix, pre,
):
    nodes, _ = grad.shape
    slots, tb, kt = send.shape[1], tiles.shape[2], tiles.shape[1]
    hid = slope.shape[1]
    for m, (d, returned) in enumerate(zip(send_order(meta), (t0, t1, t2, t3))):
        hot[:, m * slots : (m + 1) * slots] = put(live_row(send, counts, d), nodes)
        back[m * slots : (m + 1) * slots, :] = returned[...]
    acc[...] = dot(hot[...], back[...])
    for r in range(tiles.shape[0]):
        lhs = jnp.concatenate([tiles[r, k] for k in range(kt)], axis=1)
        spread = dot(lhs, grad[r * tb : (r + 1) * tb, :], 0, 0)
        for k in range(kt):
            at = pl.ds(pl.multiple_of(col[r, k] * tb, tb), tb)
            acc[at, :] += spread[k * tb : (k + 1) * tb, :]
    mix[...] = acc[...].astype(BF)
    rows = 256

    def block(i, carry):
        at = pl.ds(pl.multiple_of(i * rows, rows), rows)
        act = dot(mix[at, :], w_cls[...], 1, 1)
        pre[at, :] = (act * slope[at, :].astype(F32)).astype(BF)
        return carry

    lax.fori_loop(0, nodes // rows, block, 0)
    lhs = jnp.concatenate([top[...], bottom[...]], axis=0)
    both = dot(lhs, pre[...], 0, 0)
    half = both.shape[0] // 2
    mine[:, :hid] = both[:half]
    theirs[:, :hid] = both[half:].astype(BF)
    mine[:, hid:] = dot(hidden[meta[2] * 2 + meta[0]], mix[...], 0, 0)
    theirs[:, hid:] = dot(hidden[meta[2] * 2 + 1 - meta[0]], mix[...], 0, 0).astype(BF)


def call(kernel, scalars, arrays, outs, scratch):
    if not INTERPRET:
        arrays = [pltpu.with_memory_space_constraint(x, pltpu.VMEM) for x in arrays]
    return pl.pallas_call(
        kernel,
        in_specs=[pl.BlockSpec(memory_space=pltpu.SMEM) for _ in scalars]
        + [pl.BlockSpec(memory_space=pltpu.VMEM) for _ in arrays],
        out_specs=[pl.BlockSpec(memory_space=pltpu.VMEM) for _ in outs],
        scratch_shapes=[pltpu.VMEM(s, t) for s, t in scratch],
        out_shape=[
            jax.ShapeDtypeStruct(s, t) if INTERPRET else pltpu.VMEM(s, t) for s, t in outs
        ],
        compiler_params=pltpu.CompilerParams(vmem_limit_bytes=24 * 2**20),
        interpret=INTERPRET,
    )(*scalars, *arrays)


def work(
    features,
    adj_tiles,
    col_block,
    send_rows,
    send_counts,
    recv_target,
    edge_weight,
    labels,
    w_hidden,
    w_classes,
):
    nodes, width = features.shape
    slots = send_rows.shape[1]
    hid, classes = w_hidden.shape[1], w_classes.shape[1]
    half = w_hidden.shape[0] // 2
    n_af = lax.axis_size("af")
    n_plane = lax.axis_size("z") * lax.axis_size("gy")
    core = lax.axis_index("core")
    af = lax.axis_index("af")
    meta = jnp.stack([core, lax.axis_index("gy"), af]).astype(jnp.int32)
    swap = [(0, 1), (1, 0)]
    both = hid + classes
    part = nodes // 2

    *out, w_mine, w_other = call(
        send_kernel,
        (meta, send_counts),
        (features, send_rows, w_hidden, w_classes),
        [((slots, width), BF)] * 4 + [((half, both), BF)] * 2,
        [((slots, nodes), BF)],
    )
    arrived = trade(out)
    w_mine = [w_mine] + [turn(w_mine, "af", k) for k in range(1, n_af)]
    w_other = [w_other] + [lax.ppermute(w_mine[k], "core", swap) for k in range(1, n_af)]
    top, bottom = call(
        mix_kernel,
        (meta, col_block),
        (features, adj_tiles, *arrived, recv_target, edge_weight),
        [((part, width), BF)] * 2,
        [((nodes, 4 * slots), BF), ((4 * slots, 2 * width), BF)],
    )
    lo_t, hi_b = turn(top, "af", 1), turn(bottom, "af", -1)
    lo_b, hi_t = turn(bottom, "af", 1), turn(top, "af", -1)
    far_t, far_b = turn(lo_t, "af", 1), turn(hi_b, "af", -1)
    hidden, slope, z_pair, w_cls, *out = call(
        hidden_kernel,
        (meta, send_counts),
        (send_rows, top, bottom, lo_t, lo_b, hi_t, hi_b, far_t, far_b, *w_mine, *w_other),
        [
            ((hid // LANES, nodes, LANES), BF),
            ((nodes, hid), BF),
            ((nodes, 2 * classes), BF),
            ((hid, classes), BF),
        ]
        + [((slots, classes), BF)] * 4,
        [((n_af * 2 * half, hid), BF), ((slots, nodes), BF)],
    )
    arrived = trade(out)
    grad, *out = call(
        loss_kernel,
        (meta, col_block),
        (adj_tiles, z_pair, *arrived, recv_target, edge_weight, labels.reshape(-1, LANES)),
        [((nodes, classes), BF)] + [((slots, classes), BF)] * 4,
        [((nodes, 4 * slots), BF), ((4 * slots, 2 * classes), BF), ((slots, nodes), BF)],
    )
    returned = trade(out)
    theirs, mine = call(
        grads_kernel,
        (meta, col_block, send_counts),
        (adj_tiles, grad, *returned, send_rows, w_cls, slope, top, bottom, hidden),
        [((half, both), BF), ((half, both), F32)],
        [
            ((nodes, 4 * slots), BF),
            ((4 * slots, classes), BF),
            ((nodes, classes), F32),
            ((nodes, classes), BF),
            ((nodes, hid), BF),
        ],
    )
    total = mine + lax.ppermute(theirs, "core", swap).astype(F32)
    pieces = total.astype(BF).reshape(n_plane, half // n_plane, both)
    pieces = lax.all_to_all(pieces, PLANE, 0, 0, tiled=True)
    piece = jnp.sum(pieces.astype(F32), axis=0).astype(BF)
    mine = lax.all_to_all(
        jnp.broadcast_to(piece[None], (n_plane,) + piece.shape), PLANE, 0, 0, tiled=True
    ).reshape(half, both)
    other = lax.ppermute(mine, "core", swap)
    first = jnp.where(core == 0, mine, other)
    second = jnp.where(core == 0, other, mine)
    return (
        jnp.concatenate([first[:, :hid], second[:, :hid]], axis=0).astype(F32),
        jnp.concatenate([first[:, hid:], second[:, hid:]], axis=0).astype(F32),
    )


def solution(mesh):
    shape = mesh.devices.shape
    split = Mesh(
        np.reshape(mesh.devices, (shape[0] // 2, 2) + shape[1:]), ("z", "core", "gy", "af")
    )
    parts = ("z", "core", "gy")
    placed = (
        P(parts, "af"),
        P(parts, None, None, None),
        P(parts, None),
        P(parts, None),
        P(parts),
        P(parts, None),
        P(parts, None),
        P(parts),
        P("af", None),
        P("af", None),
    )
    return jax.shard_map(
        work,
        mesh=split,
        in_specs=placed,
        out_specs=(P("af", None), P("af", None)),
        check_vma=False,
    )
```

```python
import jax
import jax.numpy as jnp
import numpy as np
from jax import lax
from jax.experimental import pallas as pl
from jax.experimental.pallas import tpu as pltpu
from jax.sharding import Mesh
from jax.sharding import PartitionSpec as P

BF = jnp.bfloat16
F32 = jnp.float32
ROWS = ("z", "core")
PLANE = ("z", "gy")
LANES = 128
INTERPRET = False


def dot(lhs, rhs, lhs_dim=1, rhs_dim=0):
    return lax.dot_general(lhs, rhs, (((lhs_dim,), (rhs_dim,)), ((), ())), preferred_element_type=F32)


def turn(field, axis, move):
    count = lax.axis_size(axis)
    return lax.ppermute(field, axis, [(i, (i + move) % count) for i in range(count)])


def pairs_at(count, first):
    pairs = []
    for i in range(first, count - 1, 2):
        pairs += [(i, i + 1), (i + 1, i)]
    return pairs


def trade(fields):
    rows, cols = lax.axis_size(ROWS), lax.axis_size("gy")
    return (
        lax.ppermute(fields[0], "core", [(0, 1), (1, 0)]),
        lax.ppermute(fields[1], ROWS, pairs_at(rows, 1)),
        lax.ppermute(fields[2], "gy", pairs_at(cols, 0)),
        lax.ppermute(fields[3], "gy", pairs_at(cols, 1)),
    )


def send_order(meta):
    core, odd = meta[0], lax.rem(meta[1], 2)
    return (core, 1 - core, 2 + odd, 3 - odd)


def recv_order(meta):
    core, odd = meta[0], lax.rem(meta[1], 2)
    return (1 - core, core, 3 - odd, 2 + odd)


def down(row):
    return jnp.transpose(jnp.broadcast_to(row.astype(F32), (LANES, LANES)))


def pick(row, nodes, out_ref):
    lane = lax.broadcasted_iota(jnp.int32, (LANES, LANES), 1).astype(F32)
    for b in range(row.shape[1] // LANES):
        at = down(row[:, b * LANES : (b + 1) * LANES])
        for j in range(nodes // LANES):
            out_ref[b * LANES : (b + 1) * LANES, j * LANES : (j + 1) * LANES] = jnp.where(
                at == lane + float(j * LANES), 1.0, 0.0
            ).astype(BF)


def put(row, nodes):
    ids = lax.broadcasted_iota(jnp.int32, (nodes, row.shape[1]), 0)
    return jnp.where(ids == row, 1.0, 0.0).astype(BF)


def live_row(send_ref, meta, d):
    row = send_ref[pl.ds(d, 1), :]
    slot = lax.broadcasted_iota(jnp.int32, row.shape, 1)
    return jnp.where(slot < meta[3 + d], row, -1)


def weigh(arrived, weight_row, rhs_ref, base):
    width = arrived.shape[1]
    for b in range(weight_row.shape[1] // LANES):
        w = down(weight_row[:, b * LANES : (b + 1) * LANES])
        w = jnp.concatenate([w] * (width // LANES), axis=1)
        value = arrived[b * LANES : (b + 1) * LANES, :].astype(F32) * w
        high = value.astype(BF)
        low = (value - high.astype(F32)).astype(BF)
        rhs_ref[pl.ds(base + b * LANES, LANES), :width] = high
        rhs_ref[pl.ds(base + b * LANES, LANES), width:] = low


def send_kernel(
    meta, feat_in, send_in, w_hid, w_cls, tiles_in, recv_in, weight_in, labels_in,
    o0, o1, o2, o3, mine, other, feat, send, tiles, recv, weight, labels, hot, sems,
):
    nodes = feat.shape[0]
    half, hid = w_hid.shape[0] // 2, w_hid.shape[1]
    moves = [(send_in, send), (feat_in, feat)]
    for ref, part in ((mine, meta[0]), (other, 1 - meta[0])):
        at = pl.ds(pl.multiple_of(part * half, half), half)
        moves.append((w_hid.at[at, :], ref.at[:, :hid]))
        moves.append((w_cls.at[at, :], ref.at[:, hid:]))
    moves += [(tiles_in, tiles), (recv_in, recv), (weight_in, weight), (labels_in, labels)]
    copies = [pltpu.make_async_copy(x, y, sems.at[i]) for i, (x, y) in enumerate(moves)]
    for copy in copies:
        copy.start()
    copies[0].wait()
    copies[1].wait()
    for d, out in zip(send_order(meta), (o0, o1, o2, o3)):
        pick(live_row(send, meta, d), nodes, hot)
        out[...] = dot(hot[...], feat[...]).astype(BF)
    for copy in copies[2:]:
        copy.wait()


def near(tiles, col, field, block, tb):
    lhs = jnp.concatenate([tiles[block, k] for k in range(tiles.shape[1])], axis=1)
    rhs = jnp.concatenate(
        [
            field[pl.ds(pl.multiple_of(col[k, block] * tb, tb), tb), :]
            for k in range(tiles.shape[1])
        ],
        axis=0,
    )
    return dot(lhs, rhs)


def mix_kernel(meta, col, feat, tiles, r0, r1, r2, r3, recv, weight, top, bottom, hot, rhs):
    nodes, width = feat.shape
    slots, tb = recv.shape[1], tiles.shape[2]
    for m, (d, arrived) in enumerate(zip(recv_order(meta), (r0, r1, r2, r3))):
        hot[:, m * slots : (m + 1) * slots] = put(recv[pl.ds(d, 1), :], nodes)
        weigh(arrived[...], weight[pl.ds(d, 1), :], rhs, m * slots)
    part = nodes // 2
    first = meta[0] == 0
    for h, out in enumerate((top, bottom)):
        far = dot(hot[h * part : (h + 1) * part, :], rhs[...])
        far = far[:, :width] + far[:, width:]
        for b in range(part // tb):
            got = near(tiles, col, feat, h * (part // tb) + b, tb) + far[b * tb : (b + 1) * tb, :]
            turned = jnp.concatenate([got[:, width // 2 :], got[:, : width // 2]], axis=1)
            out[b * tb : (b + 1) * tb, :] = jnp.where(first, got, turned).astype(BF)


def hidden_kernel(
    meta, send, own_t, own_b, lo_t, lo_b, hi_t, hi_b, far_t, far_b,
    m0, m1, m2, m3, v0, v1, v2, v3,
    hidden, slope, z_pair, w_cls, o0, o1, o2, o3, w_all, hot,
):
    nodes = z_pair.shape[0]
    half = m0.shape[0]
    hid = w_all.shape[1]
    classes = w_cls.shape[1]
    n_af = w_cls.shape[0] // (2 * half)
    for i, (k, mine, other) in enumerate(((0, m0, v0), (1, m1, v1), (3, m3, v3), (2, m2, v2))):
        w_all[2 * i * half : (2 * i + 1) * half, :] = mine[:, :hid]
        w_all[(2 * i + 1) * half : (2 * i + 2) * half, :] = other[:, :hid]
        base = lax.rem(meta[2] + n_af - k, n_af) * 2
        w_cls[pl.ds(pl.multiple_of((base + meta[0]) * half, half), half), :] = mine[:, hid:]
        w_cls[pl.ds(pl.multiple_of((base + 1 - meta[0]) * half, half), half), :] = other[:, hid:]
    part = nodes // 2
    rows = 256
    for h, refs in enumerate(((own_t, lo_t, hi_t, far_t), (own_b, lo_b, hi_b, far_b))):

        def block(i, carry, h=h, refs=refs):
            at = pl.multiple_of(i * rows, rows)
            to = pl.multiple_of(h * part + i * rows, rows)
            lhs = jnp.concatenate([ref[pl.ds(at, rows), :] for ref in refs], axis=1)
            pre = dot(lhs, w_all[...])
            sig = jax.nn.sigmoid(pre)
            act = (pre * sig).astype(BF)
            slope[pl.ds(to, rows), :] = (sig * (1.0 + pre * (1.0 - sig))).astype(BF)
            for j in range(hid // LANES):
                hidden[j, pl.ds(to, rows), :] = act[:, j * LANES : (j + 1) * LANES]
            z = dot(act, w_cls[...])
            high = z.astype(BF)
            z_pair[pl.ds(to, rows), :classes] = high
            z_pair[pl.ds(to, rows), classes:] = (z - high.astype(F32)).astype(BF)
            return carry

        lax.fori_loop(0, part // rows, block, 0)
    for d, out in zip(send_order(meta), (o0, o1, o2, o3)):
        pick(live_row(send, meta, d), nodes, hot)
        out[...] = dot(hot[...], z_pair[:, :classes]).astype(BF)


def loss_kernel(
    meta, col, tiles, z_pair, r0, r1, r2, r3, recv, weight, labels,
    grad, b0, b1, b2, b3, hot, rhs, cols,
):
    nodes, classes = grad.shape
    slots, tb = recv.shape[1], tiles.shape[2]
    order = recv_order(meta)
    for m, (d, arrived) in enumerate(zip(order, (r0, r1, r2, r3))):
        hot[:, m * slots : (m + 1) * slots] = put(recv[pl.ds(d, 1), :], nodes)
        weigh(arrived[...], weight[pl.ds(d, 1), :], rhs, m * slots)
    part = nodes // 2
    lane = lax.broadcasted_iota(jnp.int32, (tb, classes), 1).astype(F32)
    for h in range(2):
        far = dot(hot[h * part : (h + 1) * part, :], rhs[...])
        for b in range(part // tb):
            r = h * (part // tb) + b
            logit = near(tiles, col, z_pair, r, tb) + far[b * tb : (b + 1) * tb, :]
            logit = logit[:, :classes] + logit[:, classes:]
            exponent = jnp.exp(logit - jnp.max(logit, axis=1, keepdims=True))
            probability = exponent / jnp.sum(exponent, axis=1, keepdims=True)
            onehot = jnp.where(down(labels[r : r + 1, :]) == lane, 1.0, 0.0)
            grad[r * tb : (r + 1) * tb, :] = ((probability - onehot) * (1.0 / 64.0)).astype(BF)
    for d, out in zip(order, (b0, b1, b2, b3)):
        pick(recv[pl.ds(d, 1), :], nodes, cols)
        taken = dot(cols[...], grad[...])
        row = weight[pl.ds(d, 1), :]
        for b in range(slots // LANES):
            at = slice(b * LANES, (b + 1) * LANES)
            out[at, :] = (taken[at, :] * down(row[:, at])).astype(BF)


def grads_kernel(
    meta, col, tiles, grad, t0, t1, t2, t3, send, w_cls, slope, top, bottom,
    hidden, theirs, mine, hot, back, acc, mix, pre,
):
    nodes, _ = grad.shape
    slots, tb, kt = send.shape[1], tiles.shape[2], tiles.shape[1]
    hid = slope.shape[1]
    for m, (d, returned) in enumerate(zip(send_order(meta), (t0, t1, t2, t3))):
        hot[:, m * slots : (m + 1) * slots] = put(live_row(send, meta, d), nodes)
        back[m * slots : (m + 1) * slots, :] = returned[...]
    acc[...] = dot(hot[...], back[...])
    for r in range(tiles.shape[0]):
        lhs = jnp.concatenate([tiles[r, k] for k in range(kt)], axis=1)
        spread = dot(lhs, grad[r * tb : (r + 1) * tb, :], 0, 0)
        for k in range(kt):
            at = pl.ds(pl.multiple_of(col[k, r] * tb, tb), tb)
            acc[at, :] += spread[k * tb : (k + 1) * tb, :]
    mix[...] = acc[...].astype(BF)
    rows = 256

    def block(i, carry):
        at = pl.ds(pl.multiple_of(i * rows, rows), rows)
        act = dot(mix[at, :], w_cls[...], 1, 1)
        pre[at, :] = (act * slope[at, :].astype(F32)).astype(BF)
        return carry

    lax.fori_loop(0, nodes // rows, block, 0)
    lhs = jnp.concatenate([top[...], bottom[...]], axis=0)
    both = dot(lhs, pre[...], 0, 0)
    half = both.shape[0] // 2
    mine[:, :hid] = both[:half]
    theirs[:, :hid] = both[half:].astype(BF)
    mine[:, hid:] = dot(hidden[meta[2] * 2 + meta[0]], mix[...], 0, 0)
    theirs[:, hid:] = dot(hidden[meta[2] * 2 + 1 - meta[0]], mix[...], 0, 0).astype(BF)


def call(kernel, scalars, arrays, outs, scratch, copies=0):
    space = pltpu.HBM if copies else pltpu.VMEM
    if INTERPRET:
        space = pl.ANY if copies else pltpu.VMEM
    else:
        arrays = [pltpu.with_memory_space_constraint(x, space) for x in arrays]
    sems = [pltpu.SemaphoreType.DMA((copies,))] if copies else []
    return pl.pallas_call(
        kernel,
        in_specs=[pl.BlockSpec(memory_space=pltpu.SMEM) for _ in scalars]
        + [pl.BlockSpec(memory_space=space) for _ in arrays],
        out_specs=[pl.BlockSpec(memory_space=pltpu.VMEM) for _ in outs],
        scratch_shapes=[pltpu.VMEM(s, t) for s, t in scratch] + sems,
        out_shape=[
            jax.ShapeDtypeStruct(s, t) if INTERPRET else pltpu.VMEM(s, t) for s, t in outs
        ],
        compiler_params=pltpu.CompilerParams(vmem_limit_bytes=24 * 2**20),
        interpret=INTERPRET,
    )(*scalars, *arrays)


def work(
    features,
    adj_tiles,
    col_block,
    send_rows,
    send_counts,
    recv_target,
    edge_weight,
    labels,
    w_hidden,
    w_classes,
):
    nodes, width = features.shape
    slots = send_rows.shape[1]
    hid, classes = w_hidden.shape[1], w_classes.shape[1]
    half = w_hidden.shape[0] // 2
    n_af = lax.axis_size("af")
    n_plane = lax.axis_size("z") * lax.axis_size("gy")
    core = lax.axis_index("core")
    af = lax.axis_index("af")
    place = jnp.stack([core, lax.axis_index("gy"), af]).astype(jnp.int32)
    meta = jnp.concatenate([place, send_counts])
    columns = col_block.T
    swap = [(0, 1), (1, 0)]
    both = hid + classes
    part = nodes // 2

    taken = (
        features,
        send_rows,
        w_hidden,
        w_classes,
        adj_tiles,
        recv_target,
        edge_weight,
        labels.reshape(-1, LANES),
    )
    *out, w_mine, w_other, features, send_rows, adj_tiles, recv_target, edge_weight, labels = call(
        send_kernel,
        (meta,),
        taken,
        [((slots, width), BF)] * 4
        + [((half, both), BF)] * 2
        + [(taken[i].shape, taken[i].dtype) for i in (0, 1, 4, 5, 6, 7)],
        [((slots, nodes), BF)],
        10,
    )
    arrived = trade(out)
    w_mine = [w_mine] + [turn(w_mine, "af", k) for k in range(1, n_af)]
    w_other = [w_other] + [lax.ppermute(w_mine[k], "core", swap) for k in range(1, n_af)]
    top, bottom = call(
        mix_kernel,
        (meta, columns),
        (features, adj_tiles, *arrived, recv_target, edge_weight),
        [((part, width), BF)] * 2,
        [((nodes, 4 * slots), BF), ((4 * slots, 2 * width), BF)],
    )
    lo_t, hi_b = turn(top, "af", 1), turn(bottom, "af", -1)
    lo_b, hi_t = turn(bottom, "af", 1), turn(top, "af", -1)
    far_t, far_b = turn(lo_t, "af", 1), turn(hi_b, "af", -1)
    hidden, slope, z_pair, w_cls, *out = call(
        hidden_kernel,
        (meta,),
        (send_rows, top, bottom, lo_t, lo_b, hi_t, hi_b, far_t, far_b, *w_mine, *w_other),
        [
            ((hid // LANES, nodes, LANES), BF),
            ((nodes, hid), BF),
            ((nodes, 2 * classes), BF),
            ((hid, classes), BF),
        ]
        + [((slots, classes), BF)] * 4,
        [((n_af * 2 * half, hid), BF), ((slots, nodes), BF)],
    )
    arrived = trade(out)
    grad, *out = call(
        loss_kernel,
        (meta, columns),
        (adj_tiles, z_pair, *arrived, recv_target, edge_weight, labels),
        [((nodes, classes), BF)] + [((slots, classes), BF)] * 4,
        [((nodes, 4 * slots), BF), ((4 * slots, 2 * classes), BF), ((slots, nodes), BF)],
    )
    returned = trade(out)
    theirs, mine = call(
        grads_kernel,
        (meta, columns),
        (adj_tiles, grad, *returned, send_rows, w_cls, slope, top, bottom, hidden),
        [((half, both), BF), ((half, both), F32)],
        [
            ((nodes, 4 * slots), BF),
            ((4 * slots, classes), BF),
            ((nodes, classes), F32),
            ((nodes, classes), BF),
            ((nodes, hid), BF),
        ],
    )
    total = mine + lax.ppermute(theirs, "core", swap).astype(F32)
    pieces = total.astype(BF).reshape(n_plane, half // n_plane, both)
    pieces = lax.all_to_all(pieces, PLANE, 0, 0, tiled=True)
    piece = jnp.sum(pieces.astype(F32), axis=0).astype(BF)
    mine = lax.all_to_all(
        jnp.broadcast_to(piece[None], (n_plane,) + piece.shape), PLANE, 0, 0, tiled=True
    ).reshape(half, both)
    other = lax.ppermute(mine, "core", swap)
    first = jnp.where(core == 0, mine, other)
    second = jnp.where(core == 0, other, mine)
    return (
        jnp.concatenate([first[:, :hid], second[:, :hid]], axis=0).astype(F32),
        jnp.concatenate([first[:, hid:], second[:, hid:]], axis=0).astype(F32),
    )


def solution(mesh):
    shape = mesh.devices.shape
    split = Mesh(
        np.reshape(mesh.devices, (shape[0] // 2, 2) + shape[1:]), ("z", "core", "gy", "af")
    )
    parts = ("z", "core", "gy")
    placed = (
        P(parts, "af"),
        P(parts, None, None, None),
        P(parts, None),
        P(parts, None),
        P(parts),
        P(parts, None),
        P(parts, None),
        P(parts),
        P("af", None),
        P("af", None),
    )
    return jax.shard_map(
        work,
        mesh=split,
        in_specs=placed,
        out_specs=(P("af", None), P("af", None)),
        check_vma=False,
    )
```

```python
import jax
import jax.numpy as jnp
import numpy as np
from jax import lax
from jax.experimental import pallas as pl
from jax.experimental.pallas import tpu as pltpu
from jax.sharding import Mesh
from jax.sharding import PartitionSpec as P

BF = jnp.bfloat16
F32 = jnp.float32
ROWS = ("z", "core")
PLANE = ("z", "gy")
LANES = 128
INTERPRET = False


def dot(lhs, rhs, lhs_dim=1, rhs_dim=0):
    return lax.dot_general(lhs, rhs, (((lhs_dim,), (rhs_dim,)), ((), ())), preferred_element_type=F32)


def turn(field, axis, move):
    count = lax.axis_size(axis)
    return lax.ppermute(field, axis, [(i, (i + move) % count) for i in range(count)])


def pairs_at(count, first):
    pairs = []
    for i in range(first, count - 1, 2):
        pairs += [(i, i + 1), (i + 1, i)]
    return pairs


def trade(fields):
    rows, cols = lax.axis_size(ROWS), lax.axis_size("gy")
    return (
        lax.ppermute(fields[0], "core", [(0, 1), (1, 0)]),
        lax.ppermute(fields[1], ROWS, pairs_at(rows, 1)),
        lax.ppermute(fields[2], "gy", pairs_at(cols, 0)),
        lax.ppermute(fields[3], "gy", pairs_at(cols, 1)),
    )


def send_order(meta):
    core, odd = meta[0], lax.rem(meta[1], 2)
    return (core, 1 - core, 2 + odd, 3 - odd)


def recv_order(meta):
    core, odd = meta[0], lax.rem(meta[1], 2)
    return (1 - core, core, 3 - odd, 2 + odd)


def down(row):
    return jnp.transpose(jnp.broadcast_to(row.astype(F32), (LANES, LANES)))


def pick(row, nodes, out_ref):
    lane = lax.broadcasted_iota(jnp.int32, (LANES, LANES), 1).astype(F32)
    for b in range(row.shape[1] // LANES):
        at = down(row[:, b * LANES : (b + 1) * LANES])
        for j in range(nodes // LANES):
            out_ref[b * LANES : (b + 1) * LANES, j * LANES : (j + 1) * LANES] = jnp.where(
                at == lane + float(j * LANES), 1.0, 0.0
            ).astype(BF)


def put(row, nodes):
    ids = lax.broadcasted_iota(jnp.int32, (nodes, row.shape[1]), 0)
    return jnp.where(ids == row, 1.0, 0.0).astype(BF)


def live_row(send_ref, meta, d):
    row = send_ref[pl.ds(d, 1), :]
    slot = lax.broadcasted_iota(jnp.int32, row.shape, 1)
    return jnp.where(slot < meta[3 + d], row, -1)


def weigh(arrived, weight_row, rhs_ref, base):
    width = arrived.shape[1]
    for b in range(weight_row.shape[1] // LANES):
        w = down(weight_row[:, b * LANES : (b + 1) * LANES])
        w = jnp.concatenate([w] * (width // LANES), axis=1)
        value = arrived[b * LANES : (b + 1) * LANES, :].astype(F32) * w
        high = value.astype(BF)
        low = (value - high.astype(F32)).astype(BF)
        rhs_ref[pl.ds(base + b * LANES, LANES), :width] = high
        rhs_ref[pl.ds(base + b * LANES, LANES), width:] = low


def send_kernel(
    meta, feat_in, send_in, w_hid, w_cls, tiles_in, recv_in, weight_in, labels_in,
    o0, o1, o2, o3, mine, other, quarter, feat, send, tiles, recv, weight, labels, hot, sems,
):
    nodes = feat.shape[0]
    half, hid = w_hid.shape[0] // 2, w_hid.shape[1]
    moves = [(send_in, send), (feat_in, feat)]
    for ref, part in ((mine, meta[0]), (other, 1 - meta[0])):
        at = pl.ds(pl.multiple_of(part * half, half), half)
        moves.append((w_hid.at[at, :], ref.at[:, :hid]))
        moves.append((w_cls.at[at, :], ref.at[:, hid:]))
    rows = half // 2
    at = pl.ds(pl.multiple_of(meta[0] * half + lax.rem(meta[1], 2) * rows, rows), rows)
    moves.append((w_hid.at[at, :], quarter.at[:, :hid]))
    moves.append((w_cls.at[at, :], quarter.at[:, hid:]))
    moves += [(tiles_in, tiles), (recv_in, recv), (weight_in, weight), (labels_in, labels)]
    copies = [pltpu.make_async_copy(x, y, sems.at[i]) for i, (x, y) in enumerate(moves)]
    for copy in copies:
        copy.start()
    copies[0].wait()
    copies[1].wait()
    for d, out in zip(send_order(meta), (o0, o1, o2, o3)):
        pick(live_row(send, meta, d), nodes, hot)
        out[...] = dot(hot[...], feat[...]).astype(BF)
    for copy in copies[2:]:
        copy.wait()


def near(tiles, col, field, block, tb):
    lhs = jnp.concatenate([tiles[block, k] for k in range(tiles.shape[1])], axis=1)
    rhs = jnp.concatenate(
        [
            field[pl.ds(pl.multiple_of(col[k, block] * tb, tb), tb), :]
            for k in range(tiles.shape[1])
        ],
        axis=0,
    )
    return dot(lhs, rhs)


def mix_kernel(meta, col, feat, tiles, r0, r1, r2, r3, recv, weight, top, bottom, hot, rhs):
    nodes, width = feat.shape
    slots, tb = recv.shape[1], tiles.shape[2]
    for m, (d, arrived) in enumerate(zip(recv_order(meta), (r0, r1, r2, r3))):
        hot[:, m * slots : (m + 1) * slots] = put(recv[pl.ds(d, 1), :], nodes)
        weigh(arrived[...], weight[pl.ds(d, 1), :], rhs, m * slots)
    part = nodes // 2
    first = meta[0] == 0
    for h, out in enumerate((top, bottom)):
        far = dot(hot[h * part : (h + 1) * part, :], rhs[...])
        far = far[:, :width] + far[:, width:]
        for b in range(part // tb):
            got = near(tiles, col, feat, h * (part // tb) + b, tb) + far[b * tb : (b + 1) * tb, :]
            turned = jnp.concatenate([got[:, width // 2 :], got[:, : width // 2]], axis=1)
            out[b * tb : (b + 1) * tb, :] = jnp.where(first, got, turned).astype(BF)


def hidden_kernel(
    meta, send, own_t, own_b, lo_t, lo_b, hi_t, hi_b, far_t, far_b,
    mine, other, near_w, far_w,
    hidden, slope, z_pair, w_cls, o0, o1, o2, o3, w_all, hot,
):
    nodes = z_pair.shape[0]
    half = mine.shape[0]
    hid = w_all.shape[1]
    classes = w_cls.shape[1]
    n_af = w_cls.shape[0] // (2 * half)
    rows = half // 2
    odd = lax.rem(meta[1], 2)
    for i, k in enumerate((0, 1, 3, 2)):
        base = lax.rem(meta[2] + n_af - k, n_af) * 2
        for c, (whole, pieces) in enumerate(((mine, near_w), (other, far_w))):
            to_all = (2 * i + c) * half
            to_cls = (base + (meta[0] if c == 0 else 1 - meta[0])) * half
            if k == 0:
                w_all[to_all : to_all + half, :] = whole[:, :hid]
                w_cls[pl.ds(pl.multiple_of(to_cls, half), half), :] = whole[:, hid:]
                continue
            for place, start in ((odd, (k - 1) * rows), (1 - odd, (k + n_af - 2) * rows)):
                piece = pieces[start : start + rows, :]
                step = place * rows
                w_all[pl.ds(pl.multiple_of(to_all + step, rows), rows), :] = piece[:, :hid]
                w_cls[pl.ds(pl.multiple_of(to_cls + step, rows), rows), :] = piece[:, hid:]
    part = nodes // 2
    rows = 256
    for h, refs in enumerate(((own_t, lo_t, hi_t, far_t), (own_b, lo_b, hi_b, far_b))):

        def block(i, carry, h=h, refs=refs):
            at = pl.multiple_of(i * rows, rows)
            to = pl.multiple_of(h * part + i * rows, rows)
            lhs = jnp.concatenate([ref[pl.ds(at, rows), :] for ref in refs], axis=1)
            pre = dot(lhs, w_all[...])
            sig = jax.nn.sigmoid(pre)
            act = (pre * sig).astype(BF)
            slope[pl.ds(to, rows), :] = (sig * (1.0 + pre * (1.0 - sig))).astype(BF)
            for j in range(hid // LANES):
                hidden[j, pl.ds(to, rows), :] = act[:, j * LANES : (j + 1) * LANES]
            z = dot(act, w_cls[...])
            high = z.astype(BF)
            z_pair[pl.ds(to, rows), :classes] = high
            z_pair[pl.ds(to, rows), classes:] = (z - high.astype(F32)).astype(BF)
            return carry

        lax.fori_loop(0, part // rows, block, 0)
    for d, out in zip(send_order(meta), (o0, o1, o2, o3)):
        pick(live_row(send, meta, d), nodes, hot)
        out[...] = dot(hot[...], z_pair[:, :classes]).astype(BF)


def loss_kernel(
    meta, col, tiles, z_pair, r0, r1, r2, r3, recv, weight, labels,
    grad, b0, b1, b2, b3, hot, rhs, cols,
):
    nodes, classes = grad.shape
    slots, tb = recv.shape[1], tiles.shape[2]
    order = recv_order(meta)
    for m, (d, arrived) in enumerate(zip(order, (r0, r1, r2, r3))):
        hot[:, m * slots : (m + 1) * slots] = put(recv[pl.ds(d, 1), :], nodes)
        weigh(arrived[...], weight[pl.ds(d, 1), :], rhs, m * slots)
    part = nodes // 2
    lane = lax.broadcasted_iota(jnp.int32, (tb, classes), 1).astype(F32)
    for h in range(2):
        far = dot(hot[h * part : (h + 1) * part, :], rhs[...])
        for b in range(part // tb):
            r = h * (part // tb) + b
            logit = near(tiles, col, z_pair, r, tb) + far[b * tb : (b + 1) * tb, :]
            logit = logit[:, :classes] + logit[:, classes:]
            exponent = jnp.exp(logit - jnp.max(logit, axis=1, keepdims=True))
            probability = exponent / jnp.sum(exponent, axis=1, keepdims=True)
            onehot = jnp.where(down(labels[r : r + 1, :]) == lane, 1.0, 0.0)
            grad[r * tb : (r + 1) * tb, :] = ((probability - onehot) * (1.0 / 64.0)).astype(BF)
    for d, out in zip(order, (b0, b1, b2, b3)):
        pick(recv[pl.ds(d, 1), :], nodes, cols)
        taken = dot(cols[...], grad[...])
        row = weight[pl.ds(d, 1), :]
        for b in range(slots // LANES):
            at = slice(b * LANES, (b + 1) * LANES)
            out[at, :] = (taken[at, :] * down(row[:, at])).astype(BF)


def grads_kernel(
    meta, col, tiles, grad, t0, t1, t2, t3, send, w_cls, slope, top, bottom,
    hidden, theirs, mine, hot, back, acc, mix, pre,
):
    nodes, _ = grad.shape
    slots, tb, kt = send.shape[1], tiles.shape[2], tiles.shape[1]
    hid = slope.shape[1]
    for m, (d, returned) in enumerate(zip(send_order(meta), (t0, t1, t2, t3))):
        hot[:, m * slots : (m + 1) * slots] = put(live_row(send, meta, d), nodes)
        back[m * slots : (m + 1) * slots, :] = returned[...]
    acc[...] = dot(hot[...], back[...])
    for r in range(tiles.shape[0]):
        lhs = jnp.concatenate([tiles[r, k] for k in range(kt)], axis=1)
        spread = dot(lhs, grad[r * tb : (r + 1) * tb, :], 0, 0)
        for k in range(kt):
            at = pl.ds(pl.multiple_of(col[k, r] * tb, tb), tb)
            acc[at, :] += spread[k * tb : (k + 1) * tb, :]
    mix[...] = acc[...].astype(BF)
    rows = 256

    def block(i, carry):
        at = pl.ds(pl.multiple_of(i * rows, rows), rows)
        act = dot(mix[at, :], w_cls[...], 1, 1)
        pre[at, :] = (act * slope[at, :].astype(F32)).astype(BF)
        return carry

    lax.fori_loop(0, nodes // rows, block, 0)
    lhs = jnp.concatenate([top[...], bottom[...]], axis=0)
    both = dot(lhs, pre[...], 0, 0)
    half = both.shape[0] // 2
    mine[:, :hid] = both[:half]
    theirs[:, :hid] = both[half:].astype(BF)
    mine[:, hid:] = dot(hidden[meta[2] * 2 + meta[0]], mix[...], 0, 0)
    theirs[:, hid:] = dot(hidden[meta[2] * 2 + 1 - meta[0]], mix[...], 0, 0).astype(BF)


def call(kernel, scalars, arrays, outs, scratch, copies=0):
    space = pltpu.HBM if copies else pltpu.VMEM
    if INTERPRET:
        space = pl.ANY if copies else pltpu.VMEM
    else:
        arrays = [pltpu.with_memory_space_constraint(x, space) for x in arrays]
    sems = [pltpu.SemaphoreType.DMA((copies,))] if copies else []
    return pl.pallas_call(
        kernel,
        in_specs=[pl.BlockSpec(memory_space=pltpu.SMEM) for _ in scalars]
        + [pl.BlockSpec(memory_space=space) for _ in arrays],
        out_specs=[pl.BlockSpec(memory_space=pltpu.VMEM) for _ in outs],
        scratch_shapes=[pltpu.VMEM(s, t) for s, t in scratch] + sems,
        out_shape=[
            jax.ShapeDtypeStruct(s, t) if INTERPRET else pltpu.VMEM(s, t) for s, t in outs
        ],
        compiler_params=pltpu.CompilerParams(vmem_limit_bytes=24 * 2**20),
        interpret=INTERPRET,
    )(*scalars, *arrays)


def work(
    features,
    adj_tiles,
    col_block,
    send_rows,
    send_counts,
    recv_target,
    edge_weight,
    labels,
    w_hidden,
    w_classes,
):
    nodes, width = features.shape
    slots = send_rows.shape[1]
    hid, classes = w_hidden.shape[1], w_classes.shape[1]
    half = w_hidden.shape[0] // 2
    n_af = lax.axis_size("af")
    n_plane = lax.axis_size("z") * lax.axis_size("gy")
    core = lax.axis_index("core")
    af = lax.axis_index("af")
    place = jnp.stack([core, lax.axis_index("gy"), af]).astype(jnp.int32)
    meta = jnp.concatenate([place, send_counts])
    columns = col_block.T
    swap = [(0, 1), (1, 0)]
    both = hid + classes
    part = nodes // 2

    taken = (
        features,
        send_rows,
        w_hidden,
        w_classes,
        adj_tiles,
        recv_target,
        edge_weight,
        labels.reshape(-1, LANES),
    )
    *out, w_mine, w_other, w_part, features, send_rows, adj_tiles, recv_target, edge_weight, labels = call(
        send_kernel,
        (meta,),
        taken,
        [((slots, width), BF)] * 4
        + [((half, both), BF)] * 2
        + [((half // 2, both), BF)]
        + [(taken[i].shape, taken[i].dtype) for i in (0, 1, 4, 5, 6, 7)],
        [((slots, nodes), BF)],
        12,
    )
    arrived = trade(out)
    near_w = [turn(w_part, "af", k) for k in range(1, n_af)]
    top, bottom = call(
        mix_kernel,
        (meta, columns),
        (features, adj_tiles, *arrived, recv_target, edge_weight),
        [((part, width), BF)] * 2,
        [((nodes, 4 * slots), BF), ((4 * slots, 2 * width), BF)],
    )
    near_w, _ = lax.optimization_barrier((near_w, top))
    near_w = jnp.concatenate(near_w, axis=0)
    across = lax.ppermute(near_w, "gy", pairs_at(lax.axis_size("gy"), 0))
    near_w = jnp.concatenate([near_w, across], axis=0)
    far_w = lax.ppermute(near_w, "core", swap)
    lo_t, hi_b = turn(top, "af", 1), turn(bottom, "af", -1)
    lo_b, hi_t = turn(bottom, "af", 1), turn(top, "af", -1)
    far_t, far_b = turn(lo_t, "af", 1), turn(hi_b, "af", -1)
    hidden, slope, z_pair, w_cls, *out = call(
        hidden_kernel,
        (meta,),
        (send_rows, top, bottom, lo_t, lo_b, hi_t, hi_b, far_t, far_b, w_mine, w_other, near_w, far_w),
        [
            ((hid // LANES, nodes, LANES), BF),
            ((nodes, hid), BF),
            ((nodes, 2 * classes), BF),
            ((hid, classes), BF),
        ]
        + [((slots, classes), BF)] * 4,
        [((n_af * 2 * half, hid), BF), ((slots, nodes), BF)],
    )
    arrived = trade(out)
    grad, *out = call(
        loss_kernel,
        (meta, columns),
        (adj_tiles, z_pair, *arrived, recv_target, edge_weight, labels),
        [((nodes, classes), BF)] + [((slots, classes), BF)] * 4,
        [((nodes, 4 * slots), BF), ((4 * slots, 2 * classes), BF), ((slots, nodes), BF)],
    )
    returned = trade(out)
    theirs, mine = call(
        grads_kernel,
        (meta, columns),
        (adj_tiles, grad, *returned, send_rows, w_cls, slope, top, bottom, hidden),
        [((half, both), BF), ((half, both), F32)],
        [
            ((nodes, 4 * slots), BF),
            ((4 * slots, classes), BF),
            ((nodes, classes), F32),
            ((nodes, classes), BF),
            ((nodes, hid), BF),
        ],
    )
    total = mine + lax.ppermute(theirs, "core", swap).astype(F32)
    pieces = total.astype(BF).reshape(n_plane, half // n_plane, both)
    pieces = lax.all_to_all(pieces, PLANE, 0, 0, tiled=True)
    piece = jnp.sum(pieces.astype(F32), axis=0).astype(BF)
    mine = lax.all_to_all(
        jnp.broadcast_to(piece[None], (n_plane,) + piece.shape), PLANE, 0, 0, tiled=True
    ).reshape(half, both)
    other = lax.ppermute(mine, "core", swap)
    first = jnp.where(core == 0, mine, other)
    second = jnp.where(core == 0, other, mine)
    return (
        jnp.concatenate([first[:, :hid], second[:, :hid]], axis=0).astype(F32),
        jnp.concatenate([first[:, hid:], second[:, hid:]], axis=0).astype(F32),
    )


def solution(mesh):
    shape = mesh.devices.shape
    split = Mesh(
        np.reshape(mesh.devices, (shape[0] // 2, 2) + shape[1:]), ("z", "core", "gy", "af")
    )
    parts = ("z", "core", "gy")
    placed = (
        P(parts, "af"),
        P(parts, None, None, None),
        P(parts, None),
        P(parts, None),
        P(parts),
        P(parts, None),
        P(parts, None),
        P(parts),
        P("af", None),
        P("af", None),
    )
    return jax.shard_map(
        work,
        mesh=split,
        in_specs=placed,
        out_specs=(P("af", None), P("af", None)),
        check_vma=False,
    )
```
